32 devices in a mesh: dp: 16 (over z, y, x), tensor: 2 (over core).
Axes of the slice: x: 2, y: 2, z: 4, core: 2. Of those that a mesh axis runs over, the one named last changes fastest.
Arguments:
- frames: bfloat16 [16384, 1024], P(('dp', 'tensor')), may hold values from -6 to 6
- time_embed: bfloat16 [16, 1024], P('dp'), may hold values from -6 to 6
- seg_lengths: int32 [16, 4], P('dp'), may hold values from 1 to 512, 1024 in all within a row
- mod_weight: bfloat16 [1024, 6144], P(None, 'tensor'), may hold values from -0.1875 to 0.1875
- mod_bias: bfloat16 [6144], P('tensor'), may hold values from -3 to 3
- inner_weight: bfloat16 [3, 1024, 1024], P(None, None, 'tensor'), may hold values from -0.1875 to 0.1875
- inner_bias: bfloat16 [3, 1024], P(None, 'tensor'), may hold values from -3 to 3
- outer_weight: bfloat16 [1024, 1024], P('tensor'), may hold values from -1.5 to 1.5
- outer_bias: bfloat16 [1024], replicated, may hold values from -3 to 3
- up_weight: bfloat16 [1024, 2048], P(None, 'tensor'), may hold values from -0.1875 to 0.1875
- up_bias: bfloat16 [2048], P('tensor'), may hold values from -3 to 3
- down_weight: bfloat16 [2048, 1024], P('tensor'), may hold values from -0.125 to 0.125
- down_bias: bfloat16 [1024], replicated, may hold values from -3 to 3
- cotangent: bfloat16 [16384, 1024], P(('dp', 'tensor')), may hold values from -6 to 6
Outputs:
- output: bfloat16 [16384, 1024], P(('dp', 'tensor'))
- frames_grad: float32 [16384, 1024], P(('dp', 'tensor'))
- time_grad: float32 [16, 1024], P('dp')
- mod_weight_grad: float32 [1024, 6144], P(None, 'tensor')
- mod_bias_grad: float32 [6144], P('tensor')
- inner_weight_grad: float32 [3, 1024, 1024], P(None, None, 'tensor')
- inner_bias_grad: float32 [3, 1024], P(None, 'tensor')
- outer_weight_grad: float32 [1024, 1024], P('tensor')
- outer_bias_grad: float32 [1024], replicated
- up_weight_grad: float32 [1024, 2048], P(None, 'tensor')
- up_bias_grad: float32 [2048], P('tensor')
- down_weight_grad: float32 [2048, 1024], P('tensor')
- down_bias_grad: float32 [1024], replicated
The draws below stay inside these ranges and needn't reach their ends.
Inputs may be any that keep to these rules, and one draw needn't show every extreme that they name: `seg_lengths`: each row's 4 utterance lengths sum to 1024; the longest is exactly 512.
All inputs are finite; a program needn't handle non-finite values.
Results may differ from the reference program's by a relative error of at most 0.012.
The reference program's roundings to bfloat16 on the way count: a program that leaves them out, or rounds other values in their place, can miss the bound.
Values may be sent and summed in bfloat16 or wider, within the bound.
No kernel may reach another device: no remote copies, remote signals or barrier semaphores. Data moves between devices by JAX's collectives and lax.ppermute only.
A program may use at most 256 MiB of HBM per device.

```python
import math
from functools import partial
import jax
import jax.numpy as jnp
import numpy as np
from jax import lax

D = 1024
HEADS = 16
HEAD_DIM = 64
FF = 2048
ROW_LEN = 1024
NSEG = 4
SEG_MOST = 512
ROWS = 16
TOKENS = 16384


def level_of(key, shape, cuts, smallest, largest):
    factor_of = 1.0
    for axis_at, parts in cuts:
        steps = jax.random.uniform(jax.random.fold_in(jax.random.fold_in(key, 6), axis_at), (parts,), jnp.float32, smallest / len(cuts), largest / len(cuts))
        factor_of = factor_of * jnp.repeat(jnp.exp(steps), shape[axis_at] // parts).reshape((-1,) + (1,) * (len(shape) - 1 - axis_at))
    return factor_of


def length_profile(count, total, reach, slope):
    loads = [(1 << 20) // math.isqrt(grade ** slope) + 1 for grade in range(2, count + 1)]
    spare, given = total - reach - (count - 1), [1] * (count - 1)
    while spare > 0:
        candidates = [i for i in range(count - 1) if given[i] < reach]
        pool, remaining = sum([loads[i] for i in candidates]), spare
        for i in candidates:
            addition = min(reach - given[i], max(1, remaining * loads[i] // pool), spare)
            given[i] = given[i] + addition
            spare = spare - addition
    return np.array([reach] + given)


def uneven(key, amount, total, most, skew):
    if amount == 2:
        one = jax.random.randint(key, (), max(1, total - most), min(most, total - 1) + 1)
        return jnp.stack([one, total - one])
    tallies = jnp.asarray(length_profile(amount, total, most, skew), jnp.int32)
    twos = (amount - 1) // 2
    donor, taker = tallies[1:1 + 2 * twos:2], tallies[2:2 + 2 * twos:2]
    room = jnp.minimum(donor - 1, most - taker)
    shifted = jax.random.randint(jax.random.fold_in(key, 1), (twos,), 0, 1 << 20) % (room + 1)
    tallies = tallies.at[1:1 + 2 * twos:2].set(donor - shifted).at[2:2 + 2 * twos:2].set(taker + shifted)
    return tallies[jax.random.permutation(jax.random.fold_in(key, 2), amount)]


def bell_draw(key, dims, width, reach, cuts=(), held_as=jnp.bfloat16):
    level = level_of(key, dims, cuts, -0.22, 0.18) if cuts else 1.0
    drawn = jax.random.normal(key, dims, jnp.float32) * width * level
    return jnp.minimum(jnp.maximum(drawn, -reach), reach).astype(held_as)


def setup_inputs(seed: int = 0) -> dict:
    arg_keys = jax.random.split(jax.random.key(seed), 15)
    frames = bell_draw(arg_keys[0], (TOKENS, D), 1.0, 6.0, ((0, 32),))
    time_embed = bell_draw(arg_keys[1], (ROWS, D), 1.0, 6.0, ((0, 16),))
    seg_lengths = jax.vmap(lambda own: uneven(own, NSEG, ROW_LEN, SEG_MOST, 1))(jax.random.split(arg_keys[2], ROWS)).reshape((ROWS, NSEG)).astype(jnp.int32)
    mod_weight = bell_draw(arg_keys[3], (D, 6 * D), D ** -0.5, 0.1875, ((1, 2),))
    mod_bias = bell_draw(arg_keys[4], (6 * D,), 0.5, 3.0, ((0, 2),))
    inner_weight = bell_draw(arg_keys[5], (3, D, D), D ** -0.5, 0.1875, ((2, 2),))
    inner_bias = bell_draw(arg_keys[6], (3, D), 0.3, 3.0, ((1, 2),))
    outer_weight = bell_draw(arg_keys[7], (D, D), (D // 64) ** -0.5, 1.5, ((0, 2),))
    outer_bias = bell_draw(arg_keys[8], (D,), 0.3, 3.0)
    up_weight = bell_draw(arg_keys[9], (D, FF), D ** -0.5, 0.1875, ((1, 2),))
    up_bias = bell_draw(arg_keys[10], (FF,), 0.3, 3.0, ((0, 2),))
    down_weight = bell_draw(arg_keys[11], (FF, D), FF ** -0.5, 0.125, ((0, 2),))
    down_bias = bell_draw(arg_keys[12], (D,), 0.3, 3.0)
    cotangent = bell_draw(arg_keys[13], (TOKENS, D), 1.0, 6.0, ((0, 32),))
    return {"frames": frames, "time_embed": time_embed, "seg_lengths": seg_lengths, "mod_weight": mod_weight, "mod_bias": mod_bias, "inner_weight": inner_weight, "inner_bias": inner_bias, "outer_weight": outer_weight, "outer_bias": outer_bias, "up_weight": up_weight, "up_bias": up_bias, "down_weight": down_weight, "down_bias": down_bias, "cotangent": cotangent}


@jax.custom_vjp
def low(v):
    return lax.optimization_barrier(v.astype(jnp.bfloat16)).astype(jnp.float32)

@jax.custom_vjp
def low_back(v):
    return v

def low_keep(v):
    return (low(v), None)

def low_pass(kept, grad):
    return (grad,)

def back_keep(v):
    return (v, None)

def back_low(kept, grad):
    return (low(grad),)
low.defvjp(low_keep, low_pass)
low_back.defvjp(back_keep, back_low)
highest = lax.Precision.HIGHEST

def layer_norm(values):
    centred = values - lax.optimization_barrier(jnp.mean(values, axis=-1, keepdims=True))
    return centred * lax.rsqrt(lax.optimization_barrier(jnp.mean(centred * centred, axis=-1, keepdims=True)) + 1e-06)

def rotary_tables(lengths):
    frame_index = jnp.arange(ROW_LEN, dtype=jnp.int32)
    seg_ends = jnp.cumsum(lengths).astype(jnp.int32)
    segment = lax.optimization_barrier(jnp.sum((frame_index[:, None] >= seg_ends[None, :]).astype(jnp.int32), axis=1))
    starts = (seg_ends - lengths).astype(jnp.int32)
    picked = jnp.arange(NSEG, dtype=jnp.int32)[None, :] == segment[:, None]
    before = lax.optimization_barrier(jnp.sum(jnp.where(picked, starts[None, :], 0), axis=1)).astype(jnp.int32)
    position = (frame_index - before).astype(jnp.float32)
    frequency = 10000.0 ** (-jnp.arange(HEAD_DIM // 2, dtype=jnp.float32) / (HEAD_DIM // 2))
    angles = position[:, None] * frequency[None, :]
    return (segment, jnp.cos(angles), jnp.sin(angles))

def rotate(values, cosine, sine):
    halfway = values.shape[-1] // 2
    first = values[..., :halfway]
    second = values[..., halfway:]
    cosine = cosine[..., None, :]
    sine = sine[..., None, :]
    return jnp.concatenate([first * cosine - second * sine, second * cosine + first * sine], axis=-1)

def attend_block(query_block, seg_block, key_rows, val_rows, segment):
    raw = jnp.einsum('qhe,khe->hqk', query_block, key_rows, precision=highest) * HEAD_DIM ** (-0.5)
    raw = low_back(raw)
    allowed = (seg_block[:, None] == segment[None, :])[None]
    weights = low(jax.nn.softmax(jnp.where(allowed, raw, -1e+30), axis=-1))
    return jnp.einsum('hqk,khe->qhe', weights, val_rows, precision=highest)

def attend_row(inputs):
    queries, key_rows, val_rows, segment = inputs
    block_rows = min(512, ROW_LEN)
    block_count = ROW_LEN // block_rows
    block_step = jax.checkpoint(partial(attend_block, key_rows=key_rows, val_rows=val_rows, segment=segment))
    mixed = lax.map(lambda blocks: block_step(blocks[0], blocks[1]), (queries.reshape(block_count, block_rows, HEADS, HEAD_DIM), segment.reshape(block_count, block_rows)))
    return mixed.reshape(ROW_LEN, HEADS, HEAD_DIM)

def forward(frames, time_embed, mod_weight, mod_bias, inner_weight, inner_bias, outer_weight, outer_bias, up_weight, up_bias, down_weight, down_bias, segment, cosine, sine):
    row_count = time_embed.shape[0]
    acted = low(jax.nn.silu(time_embed))
    modulation = low_back(jnp.dot(acted, mod_weight, precision=highest) + mod_bias)
    pieces = [modulation[:, None, column * D:(column + 1) * D] for column in range(6)]
    shift_attend, scale_attend, gate_attend, shift_feed, scale_feed, gate_feed = pieces
    source = frames.reshape(row_count, ROW_LEN, D)
    normed = low(layer_norm(source) * (1.0 + scale_attend) + shift_attend)
    projected = jnp.einsum('rld,pde->prle', normed, inner_weight, precision=highest) + inner_bias[:, None, None, :]
    projected = low_back(projected)
    split_heads = projected.reshape(3, row_count, ROW_LEN, HEADS, HEAD_DIM)
    queries = low(rotate(split_heads[0], cosine, sine))
    key_rows = low(rotate(split_heads[1], cosine, sine))
    val_rows = low(split_heads[2])
    mixed = lax.map(jax.checkpoint(attend_row), (queries, key_rows, val_rows, segment))
    mixed = low(low_back(mixed.reshape(row_count, ROW_LEN, D)))
    attend_sum = low_back(jnp.dot(mixed, outer_weight, precision=highest) + outer_bias)
    middle = source + gate_attend * attend_sum
    normed_feed = low(layer_norm(middle) * (1.0 + scale_feed) + shift_feed)
    lifted = low_back(jnp.dot(normed_feed, up_weight, precision=highest) + up_bias)
    activated = low(jax.nn.gelu(lifted, approximate=True))
    feed_sum = low_back(jnp.dot(activated, down_weight, precision=highest) + down_bias)
    return (middle + gate_feed * feed_sum).reshape(row_count * ROW_LEN, D)

def reference(frames, time_embed, seg_lengths, mod_weight, mod_bias, inner_weight, inner_bias, outer_weight, outer_bias, up_weight, up_bias, down_weight, down_bias, cotangent):
    segment, cosine, sine = jax.vmap(rotary_tables)(seg_lengths)
    params = tuple((member.astype(jnp.float32) for member in (frames, time_embed, mod_weight, mod_bias, inner_weight, inner_bias, outer_weight, outer_bias, up_weight, up_bias, down_weight, down_bias)))

    def wrapped(*inputs):
        return forward(*inputs, segment, cosine, sine)
    output, pullback = jax.vjp(wrapped, *params)
    gradients = pullback(cotangent.astype(jnp.float32))
    return (output.astype(jnp.bfloat16), gradients[0], gradients[1], gradients[2], gradients[3], gradients[4], gradients[5], gradients[6], gradients[7], gradients[8], gradients[9], gradients[10], gradients[11])
```

```python
import functools

import jax
import jax.numpy as jnp
from jax import lax
from jax.experimental import pallas as pl
from jax.experimental.pallas import tpu as pltpu
from jax.sharding import PartitionSpec as P

HEAD_DIM = 64
PAIR = 2 * HEAD_DIM
EPS = 1e-06
F32 = jnp.float32
BF16 = jnp.bfloat16
NT = (((1,), (1,)), ((), ()))
TN = (((0,), (0,)), ((), ()))
VMEM_LIMIT = 56 * 1024 * 1024


def mm(a, b, dims=(((1,), (0,)), ((), ()))):
    return lax.dot_general(a, b, dims, preferred_element_type=F32)


def normalise(values):
    centred = values - jnp.mean(values, axis=-1, keepdims=True)
    inverse = lax.rsqrt(jnp.mean(centred * centred, axis=-1, keepdims=True) + EPS)
    return centred * inverse, inverse


def norm_back(grad, unit, inverse, scale):
    lifted = grad * (1.0 + scale)
    mean_one = jnp.mean(lifted, axis=-1, keepdims=True)
    mean_two = jnp.mean(lifted * unit, axis=-1, keepdims=True)
    return inverse * (lifted - mean_one - unit * mean_two)


def swap_halves(values):
    width = values.shape[-1]
    lane = lax.broadcasted_iota(jnp.int32, values.shape, 1)
    ahead = pltpu.roll(values, width - HEAD_DIM // 2, 1)
    behind = pltpu.roll(values, HEAD_DIM // 2, 1)
    return jnp.where(lane % HEAD_DIM < HEAD_DIM // 2, ahead, behind)


def head_mask(which, dtype):
    lane = lax.broadcasted_iota(jnp.int32, (1, PAIR), 1)
    return jnp.where(lane // HEAD_DIM == which, 1.0, 0.0).astype(dtype)


def whole(shape):
    return pl.BlockSpec(shape, lambda *_: (0,) * len(shape))


def params(*semantics):
    return pltpu.CompilerParams(dimension_semantics=semantics, vmem_limit_bytes=VMEM_LIMIT)


def cost(flops, bytes_accessed, transcendentals=0):
    return pl.CostEstimate(
        flops=int(flops), bytes_accessed=int(bytes_accessed), transcendentals=int(transcendentals)
    )


def project_body(x, shift, scale, weight, bias, cosine, sine, normed, queries, keys, vals):
    unit, _ = normalise(x[...].astype(F32))
    rounded = (unit * (1.0 + scale[...]) + shift[...]).astype(BF16)
    normed[...] = rounded
    repeats = weight.shape[2] // PAIR
    cos = jnp.concatenate([cosine[...]] * repeats, axis=1)
    sin = jnp.concatenate([sine[...]] * repeats, axis=1)
    first = mm(rounded, weight[0]) + bias[0:1, :]
    queries[...] = ((first * cos + swap_halves(first) * sin) * HEAD_DIM ** (-0.5)).astype(BF16)
    second = mm(rounded, weight[1]) + bias[1:2, :]
    keys[...] = (second * cos + swap_halves(second) * sin).astype(BF16)
    vals[...] = (mm(rounded, weight[2]) + bias[2:3, :]).astype(BF16)


def project(x, shift, scale, weight, bias, cosine, sine, block=256):
    rows, width = x.shape
    local = weight.shape[2]
    row = lambda cols: pl.BlockSpec((block, cols), lambda i: (i, 0))
    return pl.pallas_call(
        project_body,
        grid=(rows // block,),
        in_specs=[
            row(width),
            whole((1, width)),
            whole((1, width)),
            whole(weight.shape),
            whole(bias.shape),
            row(PAIR),
            row(PAIR),
        ],
        out_specs=[row(width), row(local), row(local), row(local)],
        out_shape=[jax.ShapeDtypeStruct((rows, width), BF16)]
        + [jax.ShapeDtypeStruct((rows, local), BF16)] * 3,
        compiler_params=params("arbitrary"),
        cost_estimate=cost(6 * rows * width * local, 4 * rows * width + 6 * rows * local + 6 * width * local),
        name="project",
    )(x, shift, scale, weight, bias, cosine, sine)


def attend_body(queries, keys, vals, seg_col, seg_row, mixed, logs):
    q, k, v = queries[...], keys[...], vals[...]
    allowed = seg_col[...] == seg_row[...]
    total = None
    for which in (0, 1):
        raw = mm(q * head_mask(which, BF16), k, NT)
        raw = jnp.where(allowed, raw, -1e30)
        largest = jnp.max(raw, axis=-1, keepdims=True)
        powers = jnp.exp(raw - largest)
        sums = jnp.sum(powers, axis=-1, keepdims=True)
        weights = (powers * (1.0 / sums)).astype(BF16)
        part = mm(weights, v) * head_mask(which, F32)
        total = part if total is None else total + part
        stat = jnp.broadcast_to(largest + jnp.log(sums), (q.shape[0], PAIR))
        logs[which : which + 1, :] = jnp.transpose(stat)[0:1, :]
    mixed[...] = total.astype(BF16)


def attend(queries, keys, vals, seg_col, seg_row, block=256):
    rows, local = queries.shape
    pairs = local // PAIR
    return pl.pallas_call(
        attend_body,
        grid=(pairs, rows // block),
        in_specs=[
            pl.BlockSpec((block, PAIR), lambda p, i: (i, p)),
            pl.BlockSpec((rows, PAIR), lambda p, i: (0, p)),
            pl.BlockSpec((rows, PAIR), lambda p, i: (0, p)),
            pl.BlockSpec((block, 1), lambda p, i: (i, 0)),
            whole((1, rows)),
        ],
        out_specs=[
            pl.BlockSpec((block, PAIR), lambda p, i: (i, p)),
            pl.BlockSpec((None, 8, block), lambda p, i: (p, 0, i)),
        ],
        out_shape=[
            jax.ShapeDtypeStruct((rows, local), BF16),
            jax.ShapeDtypeStruct((pairs, 8, rows), F32),
        ],
        compiler_params=params("arbitrary", "arbitrary"),
        cost_estimate=cost(16 * rows * rows * local, 8 * rows * local, 2 * pairs * rows * rows),
        name="attend",
    )(queries, keys, vals, seg_col, seg_row)


def attend_back_body(
    queries, keys, vals, grads, logs, seg_col, seg_row, cos_q, sin_q, cos_k, sin_k,
    query_grad, key_grad, val_grad, key_sum, val_sum,
):
    step = pl.program_id(1)
    q, k, v, g = queries[...], keys[...], vals[...], grads[...]

    @pl.when(step == 0)
    def _():
        key_sum[...] = jnp.zeros_like(key_sum)
        val_sum[...] = jnp.zeros_like(val_sum)

    allowed = seg_col[...] == seg_row[...]
    total = None
    for which in (0, 1):
        qh = q * head_mask(which, BF16)
        gh = g * head_mask(which, BF16)
        raw = jnp.where(allowed, mm(k, qh, NT), -1e30)
        probs = jnp.exp(raw - logs[which : which + 1, :])
        prob_grad = mm(v, gh, NT)
        centre = jnp.sum(probs * prob_grad, axis=0, keepdims=True)
        score = (probs * (prob_grad - centre)).astype(BF16)
        val_sum[...] += mm(probs.astype(BF16), gh)
        key_sum[...] += mm(score, qh)
        part = mm(score, k, TN) * head_mask(which, F32)
        total = part if total is None else total + part
    total = total * HEAD_DIM ** (-0.5)
    query_grad[...] = (total * cos_q[...] - swap_halves(total) * sin_q[...]).astype(BF16)

    @pl.when(step == pl.num_programs(1) - 1)
    def _():
        turned = key_sum[...]
        key_grad[...] = (turned * cos_k[...] - swap_halves(turned) * sin_k[...]).astype(BF16)
        val_grad[...] = val_sum[...].astype(BF16)


def attend_back(queries, keys, vals, grads, logs, seg_col, seg_row, cosine, sine, block=256):
    rows, local = queries.shape
    pairs = local // PAIR
    some = pl.BlockSpec((block, PAIR), lambda p, i: (i, p))
    full = pl.BlockSpec((rows, PAIR), lambda p, i: (0, p))
    shape = jax.ShapeDtypeStruct((rows, local), BF16)
    return pl.pallas_call(
        attend_back_body,
        grid=(pairs, rows // block),
        in_specs=[
            some,
            full,
            full,
            some,
            pl.BlockSpec((None, 8, block), lambda p, i: (p, 0, i)),
            whole((rows, 1)),
            pl.BlockSpec((1, block), lambda p, i: (0, i)),
            pl.BlockSpec((block, PAIR), lambda p, i: (i, 0)),
            pl.BlockSpec((block, PAIR), lambda p, i: (i, 0)),
            whole((rows, PAIR)),
            whole((rows, PAIR)),
        ],
        out_specs=[some, full, full],
        out_shape=[shape] * 3,
        scratch_shapes=[pltpu.VMEM((rows, PAIR), F32)] * 2,
        compiler_params=params("arbitrary", "arbitrary"),
        cost_estimate=cost(40 * rows * rows * local, 14 * rows * local, 2 * pairs * rows * rows),
        name="attend_back",
    )(queries, keys, vals, grads, logs, seg_col, seg_row, cosine, sine, cosine, sine)


def matmul_body(a, b, out):
    out[...] = mm(a[...], b[...]).astype(out.dtype)


def matmul(a, b, dtype, block=256):
    rows, inner = a.shape
    cols = b.shape[1]
    return pl.pallas_call(
        matmul_body,
        grid=(rows // block,),
        in_specs=[pl.BlockSpec((block, inner), lambda i: (i, 0)), whole(b.shape)],
        out_specs=pl.BlockSpec((block, cols), lambda i: (i, 0)),
        out_shape=jax.ShapeDtypeStruct((rows, cols), dtype),
        compiler_params=params("arbitrary"),
        cost_estimate=cost(2 * rows * inner * cols, 2 * (rows * inner + inner * cols + rows * cols)),
        name="matmul",
    )(a, b)


GELU_A = 0.7978845608028654
GELU_B = 0.044715


def feed_body(
    x, own, other, outer_bias, gate_attend, shift, scale, gate_feed, up, up_bias, down, cot,
    normed, acted, lift_grad, feed_cot, feed_part, grad_part, sums,
):
    attend_sum = own[...].astype(F32) + other[...].astype(F32) + outer_bias[...]
    middle = x[...].astype(F32) + gate_attend[...] * attend_sum
    unit, _ = normalise(middle)
    rounded = (unit * (1.0 + scale[...]) + shift[...]).astype(BF16)
    normed[...] = rounded
    lifted = mm(rounded, up[...]) + up_bias[...]
    square = lifted * lifted
    tanh = jnp.tanh(GELU_A * lifted * (1.0 + GELU_B * square))
    half = 0.5 * (1.0 + tanh)
    active = (lifted * half).astype(BF16)
    slope = half + 0.5 * lifted * (1.0 - tanh * tanh) * (GELU_A * (1.0 + 3.0 * GELU_B * square))
    acted[...] = active
    part = mm(active, down[...])
    feed_part[...] = part.astype(BF16)
    g = cot[...].astype(F32)
    fc = (gate_feed[...] * g).astype(BF16)
    feed_cot[...] = fc
    lg = (mm(fc, down[...], NT) * slope).astype(BF16)
    lift_grad[...] = lg
    grad_part[...] = mm(lg, up[...], NT).astype(BF16)
    sums[...] = jnp.zeros_like(sums)
    sums[0:1, :] = jnp.sum(g * part, axis=0, keepdims=True)
    sums[1:2, :] = jnp.sum(fc.astype(F32), axis=0, keepdims=True)
    sums[2:3, : lg.shape[1]] = jnp.sum(lg.astype(F32), axis=0, keepdims=True)


def other_half(blocks, paired):
    return (lambda i: ((i + blocks // 2) % blocks, 0)) if paired else (lambda i: (i, 0))


def feed(x, own, other, paired, outer_bias, gate_attend, shift, scale, gate_feed, up, up_bias, down, cot, block=256):
    rows, width = x.shape
    units = up.shape[1]
    blocks = rows // block
    row = lambda cols: pl.BlockSpec((block, cols), lambda i: (i, 0))
    vec = whole((1, width))
    wide = jax.ShapeDtypeStruct((rows, width), BF16)
    thin = jax.ShapeDtypeStruct((rows, units), BF16)
    return pl.pallas_call(
        feed_body,
        grid=(blocks,),
        in_specs=[
            row(width),
            row(width),
            pl.BlockSpec((block, width), other_half(blocks, paired)),
            vec, vec, vec, vec, vec,
            whole(up.shape),
            whole((1, units)),
            whole(down.shape),
            row(width),
        ],
        out_specs=[
            row(width), row(units), row(units), row(width), row(width), row(width),
            pl.BlockSpec((None, 8, width), lambda i: (i, 0, 0)),
        ],
        out_shape=[wide, thin, thin, wide, wide, wide, jax.ShapeDtypeStruct((blocks, 8, width), F32)],
        compiler_params=params("arbitrary"),
        cost_estimate=cost(8 * rows * width * units, 16 * rows * width + 4 * rows * units + 4 * width * units, rows * units),
        name="feed",
    )(x, own, other, outer_bias, gate_attend, shift, scale, gate_feed, up, up_bias, down, cot)


def middle_body(
    x, own, other, outer_bias, gate_attend, scale, grad_own, grad_other, cot, outer,
    middle_grad, attend_cot, heads_grad, sums,
):
    attend_sum = own[...].astype(F32) + other[...].astype(F32) + outer_bias[...]
    middle = x[...].astype(F32) + gate_attend[...] * attend_sum
    unit, inverse = normalise(middle)
    grad = grad_own[...].astype(F32) + grad_other[...].astype(F32)
    mg = cot[...].astype(F32) + norm_back(grad, unit, inverse, scale[...])
    middle_grad[...] = mg
    ac = (gate_attend[...] * mg).astype(BF16)
    attend_cot[...] = ac
    heads_grad[...] = mm(ac, outer[...], NT).astype(BF16)
    sums[...] = jnp.zeros_like(sums)
    sums[0:1, :] = jnp.sum(grad, axis=0, keepdims=True)
    sums[1:2, :] = jnp.sum(grad * unit, axis=0, keepdims=True)
    sums[2:3, :] = jnp.sum(mg * attend_sum, axis=0, keepdims=True)
    sums[3:4, :] = jnp.sum(ac.astype(F32), axis=0, keepdims=True)


def middle_back(x, own, other, paired, outer_bias, gate_attend, scale, grad_own, grad_other, cot, outer, block=256):
    rows, width = x.shape
    local = outer.shape[0]
    blocks = rows // block
    row = lambda cols: pl.BlockSpec((block, cols), lambda i: (i, 0))
    across = pl.BlockSpec((block, width), other_half(blocks, paired))
    vec = whole((1, width))
    return pl.pallas_call(
        middle_body,
        grid=(blocks,),
        in_specs=[row(width), row(width), across, vec, vec, vec, row(width), across, row(width), whole(outer.shape)],
        out_specs=[row(width), row(width), row(local), pl.BlockSpec((None, 8, width), lambda i: (i, 0, 0))],
        out_shape=[
            jax.ShapeDtypeStruct((rows, width), F32),
            jax.ShapeDtypeStruct((rows, width), BF16),
            jax.ShapeDtypeStruct((rows, local), BF16),
            jax.ShapeDtypeStruct((blocks, 8, width), F32),
        ],
        compiler_params=params("arbitrary"),
        cost_estimate=cost(2 * rows * width * local, 20 * rows * width),
        name="middle_back",
    )(x, own, other, outer_bias, gate_attend, scale, grad_own, grad_other, cot, outer)


def spread_body(query_grad, key_grad, val_grad, weight, out):
    total = mm(query_grad[...], weight[0], NT) + mm(key_grad[...], weight[1], NT)
    out[...] = (total + mm(val_grad[...], weight[2], NT)).astype(BF16)


def spread(query_grad, key_grad, val_grad, weight, first, count, block=256):
    local = query_grad.shape[1]
    width = weight.shape[1]
    some = pl.BlockSpec((block, local), lambda i: (i + first // block, 0))
    return pl.pallas_call(
        spread_body,
        grid=(count // block,),
        in_specs=[some, some, some, whole(weight.shape)],
        out_specs=pl.BlockSpec((block, width), lambda i: (i, 0)),
        out_shape=jax.ShapeDtypeStruct((count, width), BF16),
        compiler_params=params("arbitrary"),
        cost_estimate=cost(6 * count * local * width, 6 * (count * local + local * width) + 2 * count * width),
        name="spread",
    )(query_grad, key_grad, val_grad, weight)


def final_body(x, scale, own, other, middle_grad, frames_grad, sums):
    unit, inverse = normalise(x[...].astype(F32))
    grad = own[...].astype(F32) + other[...].astype(F32)
    frames_grad[...] = middle_grad[...] + norm_back(grad, unit, inverse, scale[...])
    sums[...] = jnp.zeros_like(sums)
    sums[0:1, :] = jnp.sum(grad, axis=0, keepdims=True)
    sums[1:2, :] = jnp.sum(grad * unit, axis=0, keepdims=True)


def final_back(x, scale, own, other, middle_grad):
    rows, width = x.shape
    block = min(256, rows)
    blocks = rows // block
    row = pl.BlockSpec((block, width), lambda i: (i, 0))
    return pl.pallas_call(
        final_body,
        grid=(blocks,),
        in_specs=[row, whole((1, width)), row, row, row],
        out_specs=[row, pl.BlockSpec((None, 8, width), lambda i: (i, 0, 0))],
        out_shape=[jax.ShapeDtypeStruct((rows, width), F32), jax.ShapeDtypeStruct((blocks, 8, width), F32)],
        compiler_params=params("arbitrary"),
        cost_estimate=cost(20 * rows * width, 14 * rows * width),
        name="final_back",
    )(x, scale, own, other, middle_grad)


def stages_of(size, flip):
    bits = [1 << b for b in range(size.bit_length() - 1)]
    if size == 16:
        pair = [[2], [1]] if flip else [[1], [2]]
        return pair + [[4, 8, 12]]
    return [[b] for b in (bits[::-1] if flip else bits)]


def place(index, masks):
    low = min(masks)
    return (index // low) % (len(masks) + 1), low


def cross(values, mask, size):
    return lax.ppermute(values, "dp", [(i, i ^ mask) for i in range(size)])


def reduce_pieces(values, stages, index, size):
    for masks in stages:
        here, low = place(index, masks)
        count = len(masks) + 1
        rows = values.shape[0] // count
        take = lambda at: lax.dynamic_slice_in_dim(values, at * rows, rows, 0)
        got = {0: take(here)}
        for mask in masks:
            got[mask] = cross(take(here ^ (mask // low)).astype(BF16), mask, size).astype(F32)
        values = add_all(got, masks)
    return values


def add_all(got, masks):
    if len(masks) == 3:
        return (got[0] + got[masks[0]]) + (got[masks[1]] + got[masks[2]])
    return got[0] + got[masks[0]]


def gather_pieces(values, stages, index, size, dtype):
    for at, masks in reversed(list(enumerate(stages))):
        here, low = place(index, masks)
        got = [values] + [cross(values, mask, size) for mask in masks]
        kind = dtype if at == 0 else values.dtype
        if len(got) == 2:
            even = here == 0
            parts = [jnp.where(even, got[0], got[1]), jnp.where(even, got[1], got[0])]
        else:
            odd, high = here % 2 == 1, here >= 2
            near = [jnp.where(odd, got[1], got[0]), jnp.where(odd, got[0], got[1])]
            far = [jnp.where(odd, got[3], got[2]), jnp.where(odd, got[2], got[3])]
            parts = [jnp.where(high, f, n) for n, f in zip(near, far)]
            parts += [jnp.where(high, n, f) for n, f in zip(near, far)]
        values = jnp.concatenate([p.astype(kind) for p in parts], axis=0)
    return values


def sum_over_dp(values, flip, index, size):
    stages = stages_of(size, flip)
    mine = reduce_pieces(values, stages, index, size).astype(BF16)
    mine = lax.optimization_barrier(mine)
    return gather_pieces(mine, stages, index, size, F32)


def small_sum(values, index, size):
    for masks in stages_of(size, False):
        got = {0: values}
        for mask in masks:
            got[mask] = cross(values, mask, size)
        values = add_all(got, masks)
    return values


def small_gather(values, size):
    for masks in stages_of(size, False):
        values = jnp.concatenate([values] + [cross(values, mask, size) for mask in masks], axis=0)
    return values


def tables(lengths, row_len, offset):
    frame_index = (jnp.arange(row_len, dtype=jnp.int32) + offset) % row_len
    seg_ends = jnp.cumsum(lengths)
    segment = jnp.sum((frame_index[:, None] >= seg_ends[None, :]).astype(jnp.int32), axis=1)
    starts = seg_ends - lengths
    picked = jnp.arange(lengths.shape[0], dtype=jnp.int32)[None, :] == segment[:, None]
    before = jnp.sum(jnp.where(picked, starts[None, :], 0), axis=1)
    position = (frame_index - before).astype(F32)
    half = HEAD_DIM // 2
    frequency = 10000.0 ** (-jnp.arange(half, dtype=F32) / half)
    angles = position[:, None] * frequency[None, :]
    cosine, sine = jnp.cos(angles), jnp.sin(angles)
    return (
        segment,
        jnp.concatenate([cosine] * 4, axis=1),
        jnp.concatenate([-sine, sine, -sine, sine], axis=1),
    )


def per_device(
    frames, time_embed, seg_lengths, mod_weight, mod_bias, inner_weight, inner_bias, outer_weight,
    outer_bias, up_weight, up_bias, down_weight, down_bias, cotangent,
):
    tok, width = frames.shape
    group = lax.axis_size("tensor")
    size = lax.axis_size("dp")
    index = lax.axis_index("dp")
    rank = lax.axis_index("tensor")
    rows = tok * group
    paired = group == 2
    swap = lambda v: lax.ppermute(v, "tensor", [(0, 1), (1, 0)])

    def all_rows(values):
        if paired:
            return jnp.concatenate([values, swap(values)], axis=0)
        return lax.all_gather(values, "tensor", axis=0, tiled=True)

    def own_rows(values):
        if paired:
            return values[:tok]
        return lax.dynamic_slice_in_dim(values, rank * tok, tok, 0)

    def both(values):
        if paired:
            return values, swap(values)
        return lax.psum(values.astype(F32), "tensor"), jnp.zeros_like(values)

    def tensor_sum(values):
        return values + swap(values) if paired else lax.psum(values, "tensor")

    x = all_rows(frames)
    cot = all_rows(cotangent)
    segment, cosine, sine = tables(seg_lengths[0], rows, rank * tok if paired else 0)
    seg_col, seg_row = segment[:, None], segment[None, :]
    acted = jax.nn.silu(time_embed.astype(F32)).astype(BF16)
    mod_part = jnp.dot(acted, mod_weight, preferred_element_type=F32) + mod_bias.astype(F32)
    if paired:
        other = swap(mod_part)
        first = rank == 0
        modulation = jnp.concatenate(
            [jnp.where(first, mod_part, other), jnp.where(first, other, mod_part)], axis=1
        )
    else:
        modulation = lax.all_gather(mod_part, "tensor", axis=1, tiled=True)
    shift_attend, scale_attend, gate_attend, shift_feed, scale_feed, gate_feed = [
        modulation[:, column * width : (column + 1) * width] for column in range(6)
    ]
    normed, queries, keys, vals = project(
        x, shift_attend, scale_attend, inner_weight, inner_bias.astype(F32), cosine, sine
    )
    mixed, logs = attend(queries, keys, vals, seg_col, seg_row)
    attend_own, attend_other = both(matmul(mixed, outer_weight, BF16))
    outer_vec = outer_bias.astype(F32)[None, :]
    normed_feed, active, lift_grad, feed_cot, feed_part, grad_part, feed_sums = feed(
        x, attend_own, attend_other, paired, outer_vec, gate_attend, shift_feed, scale_feed, gate_feed,
        up_weight, up_bias.astype(F32)[None, :], down_weight, cot,
    )
    grad_own, grad_other = both(grad_part)
    down_grad = mm(active, feed_cot, TN)
    up_grad = mm(normed_feed, lift_grad, TN)
    down_total = sum_over_dp(down_grad, False, index, size)
    up_total = sum_over_dp(up_grad, True, index, size)
    middle_grad, attend_cot, heads_grad, middle_sums = middle_back(
        x, attend_own, attend_other, paired, outer_vec, gate_attend, scale_feed,
        grad_own, grad_other, cot, outer_weight,
    )
    outer_grad = mm(mixed, attend_cot, TN)
    outer_total = sum_over_dp(outer_grad, False, index, size)

    if paired:
        feed_sum = feed_part[:tok].astype(F32) + swap(feed_part[tok:]).astype(F32)
        attend_sum = attend_own[:tok].astype(F32) + attend_other[tok:].astype(F32) + outer_vec
    else:
        feed_sum = lax.psum_scatter(feed_part.astype(F32), "tensor", scatter_dimension=0, tiled=True)
        attend_sum = own_rows(attend_own) + outer_vec
    feed_sum = feed_sum + down_bias.astype(F32)[None, :]
    output = (frames.astype(F32) + gate_attend * attend_sum + gate_feed * feed_sum).astype(BF16)

    query_grad, key_grad, val_grad = attend_back(
        queries, keys, vals, heads_grad, logs, seg_col, seg_row, cosine, sine
    )
    if paired:
        spread_other = swap(spread(query_grad, key_grad, val_grad, inner_weight, tok, tok))
        spread_own = spread(query_grad, key_grad, val_grad, inner_weight, 0, tok)
    else:
        spread_own = lax.psum_scatter(
            spread(query_grad, key_grad, val_grad, inner_weight, 0, rows).astype(F32),
            "tensor", scatter_dimension=0, tiled=True,
        )
        spread_other = jnp.zeros_like(spread_own)
    inner_grads = [mm(normed, part, TN) for part in (query_grad, key_grad, val_grad)]
    inner_total = jnp.stack(
        [sum_over_dp(part, at == 1, index, size) for at, part in enumerate(inner_grads)]
    )
    frames_grad, final_sums = final_back(
        frames, scale_attend, spread_own, spread_other, own_rows(middle_grad)
    )

    def fold(parts):
        while parts.shape[0] > 1:
            parts = parts[0::2] + parts[1::2]
        return parts[0]

    feed_vec, middle_vec, final_vec = fold(feed_sums), fold(middle_sums), fold(final_sums)
    crossing = tensor_sum(jnp.concatenate([final_vec[0:1], final_vec[1:2], feed_vec[0:1]], axis=1))
    gate_feed_grad = crossing[:, 2 * width :]
    down_bias_grad = feed_vec[1]
    gate_feed_grad = gate_feed_grad + down_bias.astype(F32)[None, :] * cot_sum(cot)
    mod_full = jnp.concatenate(
        [crossing[:, : 2 * width], middle_vec[2:3], middle_vec[0:1], middle_vec[1:2], gate_feed_grad],
        axis=1,
    )
    share = mod_weight.shape[1]
    mod_grad = lax.dynamic_slice_in_dim(mod_full, rank * share, share, 1).astype(BF16)
    gathered = small_gather(jnp.concatenate([acted, mod_grad], axis=1), size)
    all_acted, all_mod = gathered[:, :width], gathered[:, width:]
    mod_weight_grad = mm(all_acted, all_mod, TN)
    by_row = all_mod.astype(F32)
    mod_bias_grad = jnp.sum(by_row, axis=0)
    acted_grad = tensor_sum(mm(mod_grad, mod_weight, NT))
    time_grad = jax.vjp(jax.nn.silu, time_embed.astype(F32))[1](acted_grad)[0]

    local = inner_weight.shape[2]
    units = up_weight.shape[1]
    biases = small_sum(
        jnp.concatenate(
            [jnp.sum(p.astype(F32), axis=0) for p in (query_grad, key_grad, val_grad)]
            + [feed_vec[2, :units], middle_vec[3], down_bias_grad]
        )[None, :],
        index, size,
    )[0]
    cut = 3 * local
    return (
        output,
        frames_grad,
        time_grad,
        mod_weight_grad,
        mod_bias_grad,
        inner_total,
        biases[:cut].reshape(3, local),
        outer_total,
        biases[cut + units : cut + units + width],
        up_total,
        biases[cut : cut + units],
        down_total,
        biases[cut + units + width :],
    )


def cot_sum(cot):
    return jnp.sum(cot.astype(F32), axis=0, keepdims=True)


def solution(mesh):
    in_specs = (
        P(("dp", "tensor"), None),
        P("dp", None),
        P("dp", None),
        P(None, "tensor"),
        P("tensor"),
        P(None, None, "tensor"),
        P(None, "tensor"),
        P("tensor", None),
        P(),
        P(None, "tensor"),
        P("tensor"),
        P("tensor", None),
        P(),
        P(("dp", "tensor"), None),
    )
    out_specs = (
        P(("dp", "tensor"), None),
        P(("dp", "tensor"), None),
        P("dp", None),
        P(None, "tensor"),
        P("tensor"),
        P(None, None, "tensor"),
        P(None, "tensor"),
        P("tensor", None),
        P(),
        P(None, "tensor"),
        P("tensor"),
        P("tensor", None),
        P(),
    )
    return jax.shard_map(
        per_device, mesh=mesh, in_specs=in_specs, out_specs=out_specs, check_vma=False
    )
```

```python
import functools

import jax
import jax.numpy as jnp
from jax import lax
from jax.experimental import pallas as pl
from jax.experimental.pallas import tpu as pltpu
from jax.sharding import PartitionSpec as P

HEAD_DIM = 64
PAIR = 2 * HEAD_DIM
EPS = 1e-06
F32 = jnp.float32
BF16 = jnp.bfloat16
NT = (((1,), (1,)), ((), ()))
TN = (((0,), (0,)), ((), ()))
COST_SCALE = 1000
VMEM_LIMIT = 56 * 1024 * 1024


def mm(a, b, dims=(((1,), (0,)), ((), ()))):
    return lax.dot_general(a, b, dims, preferred_element_type=F32)


def normalise(values):
    centred = values - jnp.mean(values, axis=-1, keepdims=True)
    inverse = lax.rsqrt(jnp.mean(centred * centred, axis=-1, keepdims=True) + EPS)
    return centred * inverse, inverse


def norm_back(grad, unit, inverse, scale):
    lifted = grad * (1.0 + scale)
    mean_one = jnp.mean(lifted, axis=-1, keepdims=True)
    mean_two = jnp.mean(lifted * unit, axis=-1, keepdims=True)
    return inverse * (lifted - mean_one - unit * mean_two)


def swap_halves(values):
    width = values.shape[-1]
    lane = lax.broadcasted_iota(jnp.int32, values.shape, 1)
    ahead = pltpu.roll(values, width - HEAD_DIM // 2, 1)
    behind = pltpu.roll(values, HEAD_DIM // 2, 1)
    return jnp.where(lane % HEAD_DIM < HEAD_DIM // 2, ahead, behind)


def head_mask(which, dtype):
    lane = lax.broadcasted_iota(jnp.int32, (1, PAIR), 1)
    return jnp.where(lane // HEAD_DIM == which, 1.0, 0.0).astype(dtype)


def whole(shape):
    return pl.BlockSpec(shape, lambda *_: (0,) * len(shape))


def params(*semantics):
    return pltpu.CompilerParams(dimension_semantics=semantics, vmem_limit_bytes=VMEM_LIMIT)


def cost(flops, bytes_accessed, transcendentals=0):
    return pl.CostEstimate(
        flops=int(flops // COST_SCALE), bytes_accessed=int(bytes_accessed // COST_SCALE), transcendentals=0
    )


def pick(step, half, low, high):
    return jnp.where(step < half, low, high)


def low_map(half):
    return lambda i, *_: (jnp.minimum(i, half - 1), 0)


def high_map(half):
    return lambda i, *_: (jnp.maximum(i - half, 0), 0)


def project_body(low, high, shift, scale, weight, bias, cosine, sine, normed, queries, keys, vals):
    x = pick(pl.program_id(0), pl.num_programs(0) // 2, low[...], high[...])
    unit, _ = normalise(x.astype(F32))
    rounded = (unit * (1.0 + scale[...]) + shift[...]).astype(BF16)
    normed[...] = rounded
    repeats = weight.shape[2] // PAIR
    cos = jnp.concatenate([cosine[...]] * repeats, axis=1)
    sin = jnp.concatenate([sine[...]] * repeats, axis=1)
    first = mm(rounded, weight[0]) + bias[0:1, :]
    queries[...] = ((first * cos + swap_halves(first) * sin) * HEAD_DIM ** (-0.5)).astype(BF16)
    second = mm(rounded, weight[1]) + bias[1:2, :]
    keys[...] = (second * cos + swap_halves(second) * sin).astype(BF16)
    vals[...] = (mm(rounded, weight[2]) + bias[2:3, :]).astype(BF16)


def project(low, high, shift, scale, weight, bias, cosine, sine, block=256):
    rows, width = 2 * low.shape[0], low.shape[1]
    local = weight.shape[2]
    half = rows // block // 2
    row = lambda cols: pl.BlockSpec((block, cols), lambda i: (i, 0))
    return pl.pallas_call(
        project_body,
        grid=(rows // block,),
        in_specs=[
            pl.BlockSpec((block, width), low_map(half)),
            pl.BlockSpec((block, width), high_map(half)),
            whole((1, width)),
            whole((1, width)),
            whole(weight.shape),
            whole(bias.shape),
            row(PAIR),
            row(PAIR),
        ],
        out_specs=[row(width), row(local), row(local), row(local)],
        out_shape=[jax.ShapeDtypeStruct((rows, width), BF16)]
        + [jax.ShapeDtypeStruct((rows, local), BF16)] * 3,
        compiler_params=params("arbitrary"),
        cost_estimate=cost(6 * rows * width * local, 4 * rows * width + 6 * rows * local + 6 * width * local),
        name="project",
    )(low, high, shift, scale, weight, bias, cosine, sine)


def attend_body(queries, keys, vals, seg_col, seg_row, outer, mixed, logs, low, high):
    step, pair = pl.program_id(0), pl.program_id(1)
    half = pl.num_programs(0) // 2
    q, k, v = queries[...], keys[...], vals[...]
    allowed = seg_col[...] == seg_row[...]
    total = None
    for which in (0, 1):
        raw = mm(q * head_mask(which, BF16), k, NT)
        raw = jnp.where(allowed, raw, -1e30)
        largest = jnp.max(raw, axis=-1, keepdims=True)
        powers = jnp.exp(raw - largest)
        sums = jnp.sum(powers, axis=-1, keepdims=True)
        weights = (powers * (1.0 / sums)).astype(BF16)
        part = mm(weights, v) * head_mask(which, F32)
        total = part if total is None else total + part
        stat = jnp.broadcast_to(largest + jnp.log(sums), (q.shape[0], PAIR))
        logs[which : which + 1, :] = jnp.transpose(stat)[0:1, :]
    rounded = total.astype(BF16)
    mixed[...] = rounded
    grown = mm(rounded, outer[...])
    for ref, here in ((low, step < half), (high, step >= half)):

        @pl.when(jnp.logical_and(here, pair == 0))
        def _(ref=ref):
            ref[...] = grown

        @pl.when(jnp.logical_and(here, pair > 0))
        def _(ref=ref):
            ref[...] += grown


def attend(queries, keys, vals, seg_col, seg_row, outer, block=256):
    rows, local = queries.shape
    width = outer.shape[1]
    pairs = local // PAIR
    half = rows // block // 2
    part = jax.ShapeDtypeStruct((rows // 2, width), F32)
    return pl.pallas_call(
        attend_body,
        grid=(rows // block, pairs),
        in_specs=[
            pl.BlockSpec((block, PAIR), lambda i, p: (i, p)),
            pl.BlockSpec((rows, PAIR), lambda i, p: (0, p)),
            pl.BlockSpec((rows, PAIR), lambda i, p: (0, p)),
            pl.BlockSpec((block, 1), lambda i, p: (i, 0)),
            whole((1, rows)),
            pl.BlockSpec((PAIR, width), lambda i, p: (p, 0)),
        ],
        out_specs=[
            pl.BlockSpec((block, PAIR), lambda i, p: (i, p)),
            pl.BlockSpec((None, 8, block), lambda i, p: (p, 0, i)),
            pl.BlockSpec((block, width), low_map(half)),
            pl.BlockSpec((block, width), high_map(half)),
        ],
        out_shape=[
            jax.ShapeDtypeStruct((rows, local), BF16),
            jax.ShapeDtypeStruct((pairs, 8, rows), F32),
            part,
            part,
        ],
        compiler_params=params("arbitrary", "arbitrary"),
        cost_estimate=cost(20 * rows * rows * local, 8 * rows * local, 2 * pairs * rows * rows),
        name="attend",
    )(queries, keys, vals, seg_col, seg_row, outer)


def attend_back_body(
    queries, keys, vals, grads, logs, seg_col, seg_row, cos_q, sin_q, cos_k, sin_k,
    out, sums, key_sum, val_sum,
):
    step = pl.program_id(1)
    block = queries.shape[0]
    q, k, v, g = queries[...], keys[...], vals[...], grads[...]

    @pl.when(step == 0)
    def _():
        key_sum[...] = jnp.zeros_like(key_sum)
        val_sum[...] = jnp.zeros_like(val_sum)
        sums[...] = jnp.zeros_like(sums)

    allowed = seg_col[...] == seg_row[...]
    total = None
    for which in (0, 1):
        qh = q * head_mask(which, BF16)
        gh = g * head_mask(which, BF16)
        raw = jnp.where(allowed, mm(k, qh, NT), -1e30)
        probs = jnp.exp(raw - logs[which : which + 1, :])
        prob_grad = mm(v, gh, NT)
        centre = jnp.sum(probs * prob_grad, axis=0, keepdims=True)
        score = (probs * (prob_grad - centre)).astype(BF16)
        val_sum[...] += mm(probs.astype(BF16), gh)
        key_sum[...] += mm(score, qh)
        part = mm(score, k, TN) * head_mask(which, F32)
        total = part if total is None else total + part
    total = total * HEAD_DIM ** (-0.5)
    turned = (total * cos_q[...] - swap_halves(total) * sin_q[...]).astype(BF16)
    out[0, pl.ds(pl.multiple_of(step * block, block), block), :] = turned
    sums[0:1, :] += jnp.sum(turned.astype(F32), axis=0, keepdims=True)

    @pl.when(step == pl.num_programs(1) - 1)
    def _():
        total = key_sum[...]
        turned = (total * cos_k[...] - swap_halves(total) * sin_k[...]).astype(BF16)
        out[1] = turned
        sums[1:2, :] = jnp.sum(turned.astype(F32), axis=0, keepdims=True)
        plain = val_sum[...].astype(BF16)
        out[2] = plain
        sums[2:3, :] = jnp.sum(plain.astype(F32), axis=0, keepdims=True)


def attend_back(queries, keys, vals, grads, logs, seg_col, seg_row, cosine, sine, first, count, block=256):
    rows = queries.shape[0]
    some = pl.BlockSpec((block, PAIR), lambda p, i: (i, p + first))
    full = pl.BlockSpec((rows, PAIR), lambda p, i: (0, p + first))
    return pl.pallas_call(
        attend_back_body,
        grid=(count, rows // block),
        in_specs=[
            some,
            full,
            full,
            some,
            pl.BlockSpec((None, 8, block), lambda p, i: (p + first, 0, i)),
            whole((rows, 1)),
            pl.BlockSpec((1, block), lambda p, i: (0, i)),
            pl.BlockSpec((block, PAIR), lambda p, i: (i, 0)),
            pl.BlockSpec((block, PAIR), lambda p, i: (i, 0)),
            whole((rows, PAIR)),
            whole((rows, PAIR)),
        ],
        out_specs=[
            pl.BlockSpec((3, rows, PAIR), lambda p, i: (0, 0, p)),
            pl.BlockSpec((8, PAIR), lambda p, i: (0, p)),
        ],
        out_shape=[
            jax.ShapeDtypeStruct((3, rows, count * PAIR), BF16),
            jax.ShapeDtypeStruct((8, count * PAIR), F32),
        ],
        scratch_shapes=[pltpu.VMEM((rows, PAIR), F32)] * 2,
        compiler_params=params("arbitrary", "arbitrary"),
        cost_estimate=cost(40 * rows * rows * PAIR * count, 14 * rows * PAIR * count, 2 * rows * rows * count),
        name="attend_back",
    )(queries, keys, vals, grads, logs, seg_col, seg_row, cosine, sine, cosine, sine)


GELU_A = 0.7978845608028654
GELU_B = 0.044715


def feed_body(
    x, own, other, outer_bias, gate_attend, shift, scale, gate_feed, up, up_bias, down, cot, *rest
):
    normed, acted, lift_grad, feed_cot, feed_part, grad_part, sums = rest[-7:]
    attend_sum = own[...] + other[...] + outer_bias[...]
    middle = x[...].astype(F32) + gate_attend[...] * attend_sum
    unit, _ = normalise(middle)
    rounded = (unit * (1.0 + scale[...]) + shift[...]).astype(BF16)
    normed[...] = rounded
    lifted = mm(rounded, up[...]) + up_bias[...]
    square = lifted * lifted
    tanh = jnp.tanh(GELU_A * lifted * (1.0 + GELU_B * square))
    half = 0.5 * (1.0 + tanh)
    active = (lifted * half).astype(BF16)
    slope = half + 0.5 * lifted * (1.0 - tanh * tanh) * (GELU_A * (1.0 + 3.0 * GELU_B * square))
    acted[...] = active
    part = mm(active, down[...])
    feed_part[...] = part
    g = cot[...].astype(F32)
    fc = (gate_feed[...] * g).astype(BF16)
    feed_cot[...] = fc
    lg = (mm(fc, down[...], NT) * slope).astype(BF16)
    lift_grad[...] = lg
    grad_part[...] = mm(lg, up[...], NT)
    sums[...] = jnp.zeros_like(sums)
    sums[0:1, :] = jnp.sum(g * part, axis=0, keepdims=True)
    sums[1:2, :] = jnp.sum(fc.astype(F32), axis=0, keepdims=True)
    sums[2:3, : lg.shape[1]] = jnp.sum(lg.astype(F32), axis=0, keepdims=True)
    sums[3:4, :] = jnp.sum(g, axis=0, keepdims=True)


def feed(x, own, other, outer_bias, gate_attend, shift, scale, gate_feed, up, up_bias, down, cot, before, block=256):
    tok, width = x.shape
    units = up.shape[1]
    blocks = tok // block
    start = 0 if before is None else blocks
    row = pl.BlockSpec((block, width), lambda i: (i, 0))
    at = lambda cols: pl.BlockSpec((block, cols), lambda i: (i + start, 0))
    vec = whole((1, width))
    wide = jax.ShapeDtypeStruct((2 * tok, width), BF16)
    thin = jax.ShapeDtypeStruct((2 * tok, units), BF16)
    part = jax.ShapeDtypeStruct((tok, width), F32)
    before = [] if before is None else before
    return pl.pallas_call(
        feed_body,
        grid=(blocks,),
        in_specs=[
            row, row, row, vec, vec, vec, vec, vec,
            whole(up.shape), whole((1, units)), whole(down.shape), row,
        ] + [pl.BlockSpec(memory_space=pl.ANY)] * len(before),
        out_specs=[
            at(width), at(units), at(units), at(width), row, row,
            pl.BlockSpec((None, 8, width), lambda i: (i, 0, 0)),
        ],
        out_shape=[wide, thin, thin, wide, part, part, jax.ShapeDtypeStruct((blocks, 8, width), F32)],
        input_output_aliases={12 + i: i for i in range(len(before))},
        compiler_params=params("arbitrary"),
        cost_estimate=cost(8 * tok * width * units, 24 * tok * width + 4 * tok * units + 4 * width * units, tok * units),
        name="feed",
    )(x, own, other, outer_bias, gate_attend, shift, scale, gate_feed, up, up_bias, down, cot, *before)


def middle_body(
    x, own, other, outer_bias, gate_attend, scale, grad_own, grad_other, cot, outer, *rest
):
    middle_grad, attend_cot, heads_grad, sums = rest[-4:]
    attend_sum = own[...] + other[...] + outer_bias[...]
    middle = x[...].astype(F32) + gate_attend[...] * attend_sum
    unit, inverse = normalise(middle)
    grad = grad_own[...] + grad_other[...]
    mg = cot[...].astype(F32) + norm_back(grad, unit, inverse, scale[...])
    middle_grad[...] = mg.astype(middle_grad.dtype)
    ac = (gate_attend[...] * mg).astype(BF16)
    attend_cot[...] = ac
    heads_grad[...] = mm(ac, outer[...], NT).astype(BF16)
    sums[...] = jnp.zeros_like(sums)
    sums[0:1, :] = jnp.sum(grad, axis=0, keepdims=True)
    sums[1:2, :] = jnp.sum(grad * unit, axis=0, keepdims=True)
    sums[2:3, :] = jnp.sum(mg * attend_sum, axis=0, keepdims=True)
    sums[3:4, :] = jnp.sum(ac.astype(F32), axis=0, keepdims=True)


def middle_back(x, own, other, outer_bias, gate_attend, scale, grad_own, grad_other, cot, outer, upper, before, block=256):
    tok, width = x.shape
    local = outer.shape[0]
    blocks = tok // block
    start = blocks if upper else 0
    row = pl.BlockSpec((block, width), lambda i: (i, 0))
    at = lambda cols: pl.BlockSpec((block, cols), lambda i: (i + start, 0))
    vec = whole((1, width))
    return pl.pallas_call(
        middle_body,
        grid=(blocks,),
        in_specs=[row, row, row, vec, vec, vec, row, row, row, whole(outer.shape)]
        + [pl.BlockSpec(memory_space=pl.ANY)] * len(before),
        out_specs=[row, at(width), at(local), pl.BlockSpec((None, 8, width), lambda i: (i, 0, 0))],
        out_shape=[
            jax.ShapeDtypeStruct((tok, width), F32),
            jax.ShapeDtypeStruct((2 * tok, width), BF16),
            jax.ShapeDtypeStruct((2 * tok, local), BF16),
            jax.ShapeDtypeStruct((blocks, 8, width), F32),
        ],
        input_output_aliases={10 + i: 1 + i for i in range(len(before))},
        compiler_params=params("arbitrary"),
        cost_estimate=cost(2 * tok * width * local, 26 * tok * width),
        name="middle_back",
    )(x, own, other, outer_bias, gate_attend, scale, grad_own, grad_other, cot, outer, *before)


def spread_body(*refs):
    parts, weight, out = refs[:-2], refs[-2], refs[-1]
    total = None
    for j in range(3):
        grads = jnp.concatenate([part[j] for part in parts], axis=1)
        grown = mm(grads, weight[j], NT)
        total = grown if total is None else total + grown
    out[...] = total


def spread(parts, weight, first, count, block=256):
    local = weight.shape[2]
    width = weight.shape[1]
    some = lambda part: pl.BlockSpec((3, block, part.shape[2]), lambda i: (0, i + first // block, 0))
    return pl.pallas_call(
        spread_body,
        grid=(count // block,),
        in_specs=[some(part) for part in parts] + [whole(weight.shape)],
        out_specs=pl.BlockSpec((block, width), lambda i: (i, 0)),
        out_shape=jax.ShapeDtypeStruct((count, width), F32),
        compiler_params=params("arbitrary"),
        cost_estimate=cost(6 * count * local * width, 6 * (count * local + local * width) + 4 * count * width),
        name="spread",
    )(*parts, weight)


def final_body(x, scale, own, other, middle_grad, frames_grad, sums):
    unit, inverse = normalise(x[...].astype(F32))
    grad = own[...] + other[...]
    frames_grad[...] = middle_grad[...] + norm_back(grad, unit, inverse, scale[...])
    sums[...] = jnp.zeros_like(sums)
    sums[0:1, :] = jnp.sum(grad, axis=0, keepdims=True)
    sums[1:2, :] = jnp.sum(grad * unit, axis=0, keepdims=True)


def final_back(x, scale, own, other, middle_grad):
    rows, width = x.shape
    block = min(256, rows)
    blocks = rows // block
    row = pl.BlockSpec((block, width), lambda i: (i, 0))
    return pl.pallas_call(
        final_body,
        grid=(blocks,),
        in_specs=[row, whole((1, width)), row, row, row],
        out_specs=[row, pl.BlockSpec((None, 8, width), lambda i: (i, 0, 0))],
        out_shape=[jax.ShapeDtypeStruct((rows, width), F32), jax.ShapeDtypeStruct((blocks, 8, width), F32)],
        compiler_params=params("arbitrary"),
        cost_estimate=cost(20 * rows * width, 16 * rows * width),
        name="final_back",
    )(x, scale, own, other, middle_grad)


def cross(values, mask):
    return lax.ppermute(values, "dp", [(i, i ^ mask) for i in range(16)])


def crossed(sends):
    return [cross(values, mask) for values, mask in sends]


class Reduce:
    def __init__(self, values, index):
        self.index = index
        cols = values[0].shape[-1]
        self.values = [v.reshape(-1, 4, 4, v.shape[-2] // 16, cols) for v in values]
        self.rows = self.values[0].shape[3] // 2

    def take(self, mask):
        at = (self.index % 4) ^ mask
        return [lax.dynamic_index_in_dim(v, at, 2, keepdims=False) for v in self.values]

    def first(self):
        far, rows = self.take(3), self.rows
        pack = lambda part: jnp.concatenate([f[:, :, part].astype(BF16) for f in far], axis=0)
        return [(pack(slice(0, rows)), 1), (pack(slice(rows, None)), 2)]

    def second(self, got):
        rows = self.rows
        joined = lambda mask: jnp.concatenate(self.take(mask), axis=0)
        to_x, to_y = joined(1), joined(2)
        none = jnp.zeros_like(got[0])
        to_x = (to_x + jnp.concatenate([none, got[1]], axis=2).astype(F32)).astype(BF16)
        to_y = (to_y + jnp.concatenate([got[0], none], axis=2).astype(F32)).astype(BF16)
        return [(to_x, 1), (to_y, 2)]

    def third(self, got):
        self.near = jnp.concatenate(self.take(0), axis=0) + (got[0].astype(F32) + got[1].astype(F32))
        at = self.index // 4
        block = lambda mask: lax.dynamic_index_in_dim(self.near, at ^ mask, 1, keepdims=False)
        self.own = block(0)
        return [(block(mask).astype(BF16), 4 * mask) for mask in (1, 2, 3)]

    def last(self, got):
        got = [g.astype(F32) for g in got]
        return ((self.own + got[0]) + (got[1] + got[2])).astype(BF16)


class Gather:
    def __init__(self, mine, index):
        self.index, self.mine = index, mine

    def first(self):
        return [(self.mine, 4 * mask) for mask in (1, 2, 3)]

    def second(self, got):
        self.own = jnp.stack([self.mine] + got)
        return [(self.own, 1), (self.own, 2)]

    def third(self, got):
        self.side = got
        rows = self.mine.shape[1] // 2
        return [(got[1][:, :, :rows], 1), (got[0][:, :, rows:], 2)]

    def last(self, got):
        return assemble(self.index, self.own, *self.side, *got)


def assemble_body(index, own, side_x, side_y, far_low, far_high, inner, outer):
    rows, cols = own.shape[1:]
    half = rows // 2
    here = index[0] % 4
    places = [(0, slice(0, rows), own), (1, slice(0, rows), side_x), (2, slice(0, rows), side_y)]
    places += [(3, slice(0, half), far_low), (3, slice(half, rows), far_high)]
    for mask, span, ref in places:
        inner[:, here ^ mask, span, :cols] = ref[0:3].astype(F32)
        inner[:, here ^ mask, span, cols:] = ref[5:8].astype(F32)
        outer[here ^ mask, span, :cols] = ref[3].astype(F32)
        outer[here ^ mask, span, cols:] = ref[4].astype(F32)


def assemble(index, own, side_x, side_y, far_low, far_high):
    _, count, rows, cols = own.shape
    spec = lambda r: pl.BlockSpec(
        (None, count, r, cols), lambda z, index: (z ^ (index[0] // 4), 0, 0, 0)
    )
    inner, outer = pl.pallas_call(
        assemble_body,
        grid_spec=pltpu.PrefetchScalarGridSpec(
            num_scalar_prefetch=1,
            grid=(4,),
            in_specs=[spec(rows)] * 3 + [spec(rows // 2)] * 2,
            out_specs=[
                pl.BlockSpec((3, 4, rows, 2 * cols), lambda z, index: (0, z, 0, 0)),
                pl.BlockSpec((4, rows, 2 * cols), lambda z, index: (z % 2, 0, z // 2)),
            ],
        ),
        out_shape=[
            jax.ShapeDtypeStruct((3, 16, rows, 2 * cols), F32),
            jax.ShapeDtypeStruct((8, rows, 4 * cols), F32),
        ],
        compiler_params=params("arbitrary"),
        cost_estimate=cost(0, 6 * count * 16 * rows * cols),
        name="assemble",
    )(index[None], own, side_x, side_y, far_low, far_high)
    return inner.reshape(3, 16 * rows, 2 * cols), outer.reshape(8 * rows, 4 * cols)


def gather_all(mine):
    got = lax.all_gather(mine, "dp")
    _, count, rows, cols = got.shape
    return [got[:, at].astype(F32).reshape(16 * rows, cols) for at in range(count)]


def tie(*groups):
    leaves, tree = jax.tree.flatten(groups)
    held = iter(lax.optimization_barrier(tuple(v for v in leaves if hasattr(v, "dtype"))))
    return jax.tree.unflatten(tree, [next(held) if hasattr(v, "dtype") else v for v in leaves])


def fold(parts):
    while parts.shape[0] > 1:
        parts = parts[0::2] + parts[1::2]
    return parts[0]


def tables(lengths, row_len, offset):
    frame_index = (jnp.arange(row_len, dtype=jnp.int32) + offset) % row_len
    seg_ends = jnp.cumsum(lengths)
    segment = jnp.sum((frame_index[:, None] >= seg_ends[None, :]).astype(jnp.int32), axis=1)
    starts = seg_ends - lengths
    picked = jnp.arange(lengths.shape[0], dtype=jnp.int32)[None, :] == segment[:, None]
    before = jnp.sum(jnp.where(picked, starts[None, :], 0), axis=1)
    position = (frame_index - before).astype(F32)
    half = HEAD_DIM // 2
    lane = jnp.arange(PAIR, dtype=jnp.int32)
    frequency = 10000.0 ** (-(lane % half).astype(F32) / half)
    sign = jnp.where(lane % HEAD_DIM < half, -1.0, 1.0).astype(F32)
    angles = position[:, None] * frequency[None, :]
    return segment, jnp.cos(angles), jnp.sin(angles) * sign[None, :]


def per_device(
    frames, time_embed, seg_lengths, mod_weight, mod_bias, inner_weight, inner_bias, outer_weight,
    outer_bias, up_weight, up_bias, down_weight, down_bias, cotangent,
):
    own_tok, width = frames.shape
    group = lax.axis_size("tensor")
    size = lax.axis_size("dp")
    index = lax.axis_index("dp")
    rank = lax.axis_index("tensor")
    rows = own_tok * group
    tok = rows // 2
    paired = group == 2
    staged = size == 16
    pairs = inner_weight.shape[2] // PAIR
    swap = lambda v: lax.ppermute(v, "tensor", [(0, 1), (1, 0)])

    def halves(values):
        if paired:
            return values, swap(values)
        full = lax.all_gather(values, "tensor", axis=0, tiled=True)
        return full[:tok], full[tok:]

    def summed(low, high):
        if paired:
            other_low, other_high = swap(high), swap(low)
            return (low, other_low), (high, other_high)
        low, high = lax.psum((low, high), "tensor")
        none = jnp.zeros_like(low)
        return (low, none), (high, none)

    def own_rows(low, high):
        full = jnp.concatenate([low, high], axis=0)
        return lax.dynamic_slice_in_dim(full, rank * own_tok, own_tok, 0)

    def tensor_sum(values):
        return values + swap(values) if paired else lax.psum(values, "tensor")

    x_low, x_high = halves(frames)
    cot_low, cot_high = halves(cotangent)
    segment, cosine, sine = tables(seg_lengths[0], rows, rank * tok if paired else 0)
    seg_col, seg_row = segment[:, None], segment[None, :]
    acted = jax.nn.silu(time_embed.astype(F32)).astype(BF16)
    mod_part = jnp.dot(acted, mod_weight, preferred_element_type=F32) + mod_bias.astype(F32)
    if paired:
        other = swap(mod_part)
        first = rank == 0
        modulation = jnp.concatenate(
            [jnp.where(first, mod_part, other), jnp.where(first, other, mod_part)], axis=1
        )
    else:
        modulation = lax.all_gather(mod_part, "tensor", axis=1, tiled=True)
    shift_attend, scale_attend, gate_attend, shift_feed, scale_feed, gate_feed = [
        modulation[:, column * width : (column + 1) * width] for column in range(6)
    ]
    normed, queries, keys, vals = project(
        x_low, x_high, shift_attend, scale_attend, inner_weight, inner_bias.astype(F32), cosine, sine
    )
    mixed, logs, part_low, part_high = attend(queries, keys, vals, seg_col, seg_row, outer_weight)
    (own_low, other_low), (own_high, other_high) = summed(part_low, part_high)
    outer_vec = outer_bias.astype(F32)[None, :]
    feed_rest = (
        outer_vec, gate_attend, shift_feed, scale_feed, gate_feed,
        up_weight, up_bias.astype(F32)[None, :], down_weight,
    )
    *shared, feed_low, grad_low, sums_low = feed(
        x_low, own_low, other_low, *feed_rest, cot_low, None
    )
    *shared, feed_high, grad_high, sums_high = feed(
        x_high, own_high, other_high, *feed_rest, cot_high, shared
    )
    normed_feed, active, lift_grad, feed_cot = shared
    feed_vec = fold(jnp.concatenate([sums_low, sums_high]))
    (grad_low, grad_low_other), (grad_high, grad_high_other) = summed(grad_low, grad_high)
    down_grad = mm(active, feed_cot, TN)
    up_grad = mm(normed_feed, lift_grad, TN)
    middle_rest = (outer_vec, gate_attend, scale_feed)

    if staged:
        one = Reduce([down_grad, up_grad], index)
        sends = one.first()
        grad_low_other, sends = tie(grad_low_other, sends)
        got = crossed(sends)
    middle_high, *shared, vec_high = middle_back(
        x_high, own_high, other_high, *middle_rest, grad_high, grad_high_other, cot_high,
        outer_weight, True, [],
    )
    middle_low, attend_cot, heads_grad, vec_low = middle_back(
        x_low, own_low, other_low, *middle_rest, grad_low, grad_low_other, cot_low,
        outer_weight, False, shared,
    )
    if staged:
        middle_low, attend_cot, heads_grad, vec_low, vec_high, got = tie(
            middle_low, attend_cot, heads_grad, vec_low, vec_high, got
        )
        sends = one.second(got)
    middle_vec = fold(jnp.concatenate([vec_low, vec_high]))
    outer_grad = mm(mixed, attend_cot, TN)

    back = lambda grads, first, count: attend_back(
        queries, keys, vals, grads, logs, seg_col, seg_row, cosine, sine, first, count
    )
    if paired:
        feed_sum = feed_low + swap(feed_high)
        attend_sum = own_low + other_low + outer_vec
    else:
        feed_sum = own_rows(*lax.psum((feed_low, feed_high), "tensor"))
        attend_sum = own_rows(own_low, own_high) + outer_vec
    feed_sum = feed_sum + down_bias.astype(F32)[None, :]
    output = (frames.astype(F32) + gate_attend * attend_sum + gate_feed * feed_sum).astype(BF16)

    inner_grad = lambda part: [mm(normed, part[j], TN) for j in range(3)]
    if staged:
        early = pairs // 2
        heads_grad, sends = tie(heads_grad, sends)
        got = crossed(sends)
        near = back(heads_grad, 0, early)
        near, got = tie(near, got)
        sends = one.third(got)
        cols = [outer_grad[:, at : at + early * PAIR] for at in range(0, width, early * PAIR)]
        cols = [jnp.concatenate([cols[at], cols[at + 2]], axis=0) for at in (0, 1)]
        two = Reduce(inner_grad(near[0]) + cols, index)
        sends2 = two.first()
        heads_grad, sends, sends2 = tie(heads_grad, sends, sends2)
        got, got2 = crossed(sends), crossed(sends2)
        far = back(heads_grad, early, pairs - early)
        far, got, got2 = tie(far, got, got2)
        mine = one.last(got)
        down_total, up_total = gather_all(mine)
        sends2 = two.second(got2)
        three = Reduce(inner_grad(far[0]), index)
        sends3 = three.first()
        results = [near, far]
    else:
        results = [back(heads_grad, 0, pairs)]
        inner_grads = inner_grad(results[0][0])
    parts = [part for part, _ in results]
    part_sums = jnp.concatenate([sums for _, sums in results], axis=1)

    if staged:
        parts[-1], sends2, sends3, mine = tie(parts[-1], sends2, sends3, mine)
        got2, got3 = crossed(sends2), crossed(sends3)
    if paired:
        spread_other = spread(parts, inner_weight, tok, tok)
        spread_own = spread(parts, inner_weight, 0, tok)
        if staged:
            spread_own, spread_other, got2, got3 = tie(spread_own, spread_other, got2, got3)
        spread_other = swap(spread_other)
        own_middle = middle_low
    else:
        both = lax.psum(spread(parts, inner_weight, 0, rows), "tensor")
        spread_own = own_rows(both[:tok], both[tok:])
        spread_other = jnp.zeros_like(spread_own)
        own_middle = own_rows(middle_low, middle_high)
    if staged:
        sends2, sends3 = two.third(got2), three.second(got3)
        spread_own, sends2, sends3 = tie(spread_own, sends2, sends3)
        got2, got3 = crossed(sends2), crossed(sends3)
    frames_grad, final_sums = final_back(frames, scale_attend, spread_own, spread_other, own_middle)
    if staged:
        frames_grad, final_sums, got2, got3 = tie(frames_grad, final_sums, got2, got3)
    final_vec = fold(final_sums)

    crossing = tensor_sum(jnp.concatenate([final_vec[0:1], final_vec[1:2], feed_vec[0:1]], axis=1))
    gate_feed_grad = crossing[:, 2 * width :] + down_bias.astype(F32)[None, :] * feed_vec[3:4]
    mod_full = jnp.concatenate(
        [crossing[:, : 2 * width], middle_vec[2:3], middle_vec[0:1], middle_vec[1:2], gate_feed_grad],
        axis=1,
    )
    share = mod_weight.shape[1]
    local = inner_weight.shape[2]
    units = up_weight.shape[1]
    mod_grad = lax.dynamic_slice_in_dim(mod_full, rank * share, share, 1).astype(BF16)
    inner_biases = [part_sums[j] for j in range(3)]
    biases = jnp.concatenate(inner_biases + [feed_vec[2, :units], middle_vec[3], feed_vec[1]])
    small = jnp.concatenate([acted.astype(F32), mod_grad.astype(F32), biases[None, :]], axis=1)
    if staged:
        near = jnp.concatenate([small] + [cross(small, mask) for mask in (1, 2, 3)], axis=0)
        small = jnp.concatenate([near] + [cross(near, 4 * mask) for mask in (1, 2, 3)], axis=0)
        slot = jnp.arange(size, dtype=jnp.int32)
        order = ((slot[:, None] ^ index) == slot[None, :]).astype(BF16)
        factors = mm(order, small[:, : width + share].astype(BF16)).astype(BF16)
        biases = fold(small[:, width + share :][:, None, :])[0]
    else:
        small = lax.all_gather(small, "dp", axis=0, tiled=True)
        factors = small[:, : width + share].astype(BF16)
        biases = jnp.sum(small[:, width + share :], axis=0)
    all_acted, all_mod = factors[:, :width], factors[:, width:]
    mod_weight_grad = mm(all_acted, all_mod, TN)
    mod_bias_grad = jnp.sum(all_mod.astype(F32), axis=0)
    acted_grad = tensor_sum(mm(mod_grad, mod_weight, NT))
    time_grad = jax.vjp(jax.nn.silu, time_embed.astype(F32))[1](acted_grad)[0]

    if staged:
        mine2 = two.last(got2)
        mine3 = three.last(crossed(three.third(got3)))
        gather = Gather(jnp.concatenate([mine2, mine3], axis=0), index)
        got = crossed(gather.first())
        got = crossed(gather.second(got))
        got = crossed(gather.third(got))
        inner_total, outer_total = gather.last(got)
    else:
        inner_total = jnp.stack(inner_grads)
        down_total, up_total, outer_total, inner_total = lax.psum(
            (down_grad, up_grad, outer_grad, inner_total), "dp"
        )

    cut = 3 * local
    return (
        output,
        frames_grad,
        time_grad,
        mod_weight_grad,
        mod_bias_grad,
        inner_total,
        biases[:cut].reshape(3, local),
        outer_total,
        biases[cut + units : cut + units + width],
        up_total,
        biases[cut : cut + units],
        down_total,
        biases[cut + units + width :],
    )


def solution(mesh):
    in_specs = (
        P(("dp", "tensor"), None),
        P("dp", None),
        P("dp", None),
        P(None, "tensor"),
        P("tensor"),
        P(None, None, "tensor"),
        P(None, "tensor"),
        P("tensor", None),
        P(),
        P(None, "tensor"),
        P("tensor"),
        P("tensor", None),
        P(),
        P(("dp", "tensor"), None),
    )
    out_specs = (
        P(("dp", "tensor"), None),
        P(("dp", "tensor"), None),
        P("dp", None),
        P(None, "tensor"),
        P("tensor"),
        P(None, None, "tensor"),
        P(None, "tensor"),
        P("tensor", None),
        P(),
        P(None, "tensor"),
        P("tensor"),
        P("tensor", None),
        P(),
    )
    return jax.shard_map(
        per_device, mesh=mesh, in_specs=in_specs, out_specs=out_specs, check_vma=False
    )
```

```python
import functools

import jax
import jax.numpy as jnp
from jax import lax
from jax.experimental import pallas as pl
from jax.experimental.pallas import tpu as pltpu
from jax.sharding import PartitionSpec as P

HEAD_DIM = 64
PAIR = 2 * HEAD_DIM
EPS = 1e-06
F32 = jnp.float32
BF16 = jnp.bfloat16
NT = (((1,), (1,)), ((), ()))
TN = (((0,), (0,)), ((), ()))
COST_SCALE = 1000
VMEM_LIMIT = 56 * 1024 * 1024


def mm(a, b, dims=(((1,), (0,)), ((), ()))):
    return lax.dot_general(a, b, dims, preferred_element_type=F32)


def normalise(values):
    centred = values - jnp.mean(values, axis=-1, keepdims=True)
    inverse = lax.rsqrt(jnp.mean(centred * centred, axis=-1, keepdims=True) + EPS)
    return centred * inverse, inverse


def norm_back(grad, unit, inverse, scale):
    lifted = grad * (1.0 + scale)
    mean_one = jnp.mean(lifted, axis=-1, keepdims=True)
    mean_two = jnp.mean(lifted * unit, axis=-1, keepdims=True)
    return inverse * (lifted - mean_one - unit * mean_two)


def swap_halves(values):
    width = values.shape[-1]
    lane = lax.broadcasted_iota(jnp.int32, values.shape, 1)
    ahead = pltpu.roll(values, width - HEAD_DIM // 2, 1)
    behind = pltpu.roll(values, HEAD_DIM // 2, 1)
    return jnp.where(lane % HEAD_DIM < HEAD_DIM // 2, ahead, behind)


def head_mask(which, dtype):
    lane = lax.broadcasted_iota(jnp.int32, (1, PAIR), 1)
    return jnp.where(lane // HEAD_DIM == which, 1.0, 0.0).astype(dtype)


def whole(shape):
    return pl.BlockSpec(shape, lambda *_: (0,) * len(shape))


def params(*semantics):
    return pltpu.CompilerParams(dimension_semantics=semantics, vmem_limit_bytes=VMEM_LIMIT)


def cost(flops, bytes_accessed, transcendentals=0):
    return pl.CostEstimate(
        flops=int(flops // COST_SCALE), bytes_accessed=int(bytes_accessed // COST_SCALE), transcendentals=0
    )


def pick(step, half, low, high):
    return jnp.where(step < half, low, high)


def low_map(half):
    return lambda i, *_: (jnp.minimum(i, half - 1), 0)


def high_map(half):
    return lambda i, *_: (jnp.maximum(i - half, 0), 0)


def project_body(low, high, shift, scale, weight, bias, cosine, sine, normed, queries, keys, vals):
    x = pick(pl.program_id(0), pl.num_programs(0) // 2, low[...], high[...])
    unit, _ = normalise(x.astype(F32))
    rounded = (unit * (1.0 + scale[...]) + shift[...]).astype(BF16)
    normed[...] = rounded
    repeats = weight.shape[2] // PAIR
    cos = jnp.concatenate([cosine[...]] * repeats, axis=1)
    sin = jnp.concatenate([sine[...]] * repeats, axis=1)
    first = mm(rounded, weight[0]) + bias[0:1, :]
    queries[...] = ((first * cos + swap_halves(first) * sin) * HEAD_DIM ** (-0.5)).astype(BF16)
    second = mm(rounded, weight[1]) + bias[1:2, :]
    keys[...] = (second * cos + swap_halves(second) * sin).astype(BF16)
    vals[...] = (mm(rounded, weight[2]) + bias[2:3, :]).astype(BF16)


def project(low, high, shift, scale, weight, bias, cosine, sine, block=256):
    rows, width = 2 * low.shape[0], low.shape[1]
    local = weight.shape[2]
    half = rows // block // 2
    row = lambda cols: pl.BlockSpec((block, cols), lambda i: (i, 0))
    return pl.pallas_call(
        project_body,
        grid=(rows // block,),
        in_specs=[
            pl.BlockSpec((block, width), low_map(half)),
            pl.BlockSpec((block, width), high_map(half)),
            whole((1, width)),
            whole((1, width)),
            whole(weight.shape),
            whole(bias.shape),
            row(PAIR),
            row(PAIR),
        ],
        out_specs=[row(width), row(local), row(local), row(local)],
        out_shape=[jax.ShapeDtypeStruct((rows, width), BF16)]
        + [jax.ShapeDtypeStruct((rows, local), BF16)] * 3,
        compiler_params=params("arbitrary"),
        cost_estimate=cost(6 * rows * width * local, 4 * rows * width + 6 * rows * local + 6 * width * local),
        name="project",
    )(low, high, shift, scale, weight, bias, cosine, sine)


def attend_body(queries, keys, vals, seg_col, seg_row, outer, mixed, logs, low, high):
    step, pair = pl.program_id(0), pl.program_id(1)
    half = pl.num_programs(0) // 2
    q, k, v = queries[...], keys[...], vals[...]
    allowed = seg_col[...] == seg_row[...]
    total = None
    for which in (0, 1):
        raw = mm(q * head_mask(which, BF16), k, NT)
        raw = jnp.where(allowed, raw, -1e30)
        largest = jnp.max(raw, axis=-1, keepdims=True)
        powers = jnp.exp(raw - largest)
        sums = jnp.sum(powers, axis=-1, keepdims=True)
        weights = (powers * (1.0 / sums)).astype(BF16)
        part = mm(weights, v) * head_mask(which, F32)
        total = part if total is None else total + part
        stat = jnp.broadcast_to(largest + jnp.log(sums), (q.shape[0], PAIR))
        logs[which : which + 1, :] = jnp.transpose(stat)[0:1, :]
    rounded = total.astype(BF16)
    mixed[...] = rounded
    grown = mm(rounded, outer[...])
    for ref, here in ((low, step < half), (high, step >= half)):

        @pl.when(jnp.logical_and(here, pair == 0))
        def _(ref=ref):
            ref[...] = grown

        @pl.when(jnp.logical_and(here, pair > 0))
        def _(ref=ref):
            ref[...] += grown


def attend(queries, keys, vals, seg_col, seg_row, outer, block=256):
    rows, local = queries.shape
    width = outer.shape[1]
    pairs = local // PAIR
    half = rows // block // 2
    part = jax.ShapeDtypeStruct((rows // 2, width), F32)
    return pl.pallas_call(
        attend_body,
        grid=(rows // block, pairs),
        in_specs=[
            pl.BlockSpec((block, PAIR), lambda i, p: (i, p)),
            pl.BlockSpec((rows, PAIR), lambda i, p: (0, p)),
            pl.BlockSpec((rows, PAIR), lambda i, p: (0, p)),
            pl.BlockSpec((block, 1), lambda i, p: (i, 0)),
            whole((1, rows)),
            pl.BlockSpec((PAIR, width), lambda i, p: (p, 0)),
        ],
        out_specs=[
            pl.BlockSpec((block, PAIR), lambda i, p: (i, p)),
            pl.BlockSpec((None, 8, block), lambda i, p: (p, 0, i)),
            pl.BlockSpec((block, width), low_map(half)),
            pl.BlockSpec((block, width), high_map(half)),
        ],
        out_shape=[
            jax.ShapeDtypeStruct((rows, local), BF16),
            jax.ShapeDtypeStruct((pairs, 8, rows), F32),
            part,
            part,
        ],
        compiler_params=params("arbitrary", "arbitrary"),
        cost_estimate=cost(20 * rows * rows * local, 8 * rows * local, 2 * pairs * rows * rows),
        name="attend",
    )(queries, keys, vals, seg_col, seg_row, outer)


def attend_back_body(
    queries, keys, vals, grads, logs, seg_col, seg_row, cos_q, sin_q, cos_k, sin_k, *rest
):
    out, sums, key_sum, val_sum = rest[-4:]
    step = pl.program_id(1)
    block = queries.shape[0]
    q, k, v, g = queries[...], keys[...], vals[...], grads[...]

    @pl.when(step == 0)
    def _():
        key_sum[...] = jnp.zeros_like(key_sum)
        val_sum[...] = jnp.zeros_like(val_sum)
        sums[...] = jnp.zeros_like(sums)

    allowed = seg_col[...] == seg_row[...]
    total = None
    for which in (0, 1):
        qh = q * head_mask(which, BF16)
        gh = g * head_mask(which, BF16)
        raw = jnp.where(allowed, mm(k, qh, NT), -1e30)
        probs = jnp.exp(raw - logs[which : which + 1, :])
        prob_grad = mm(v, gh, NT)
        centre = jnp.sum(probs * prob_grad, axis=0, keepdims=True)
        score = (probs * (prob_grad - centre)).astype(BF16)
        val_sum[...] += mm(probs.astype(BF16), gh)
        key_sum[...] += mm(score, qh)
        part = mm(score, k, TN) * head_mask(which, F32)
        total = part if total is None else total + part
    total = total * HEAD_DIM ** (-0.5)
    turned = (total * cos_q[...] - swap_halves(total) * sin_q[...]).astype(BF16)
    out[0, pl.ds(pl.multiple_of(step * block, block), block), :] = turned
    sums[0:1, :] += jnp.sum(turned.astype(F32), axis=0, keepdims=True)

    @pl.when(step == pl.num_programs(1) - 1)
    def _():
        total = key_sum[...]
        turned = (total * cos_k[...] - swap_halves(total) * sin_k[...]).astype(BF16)
        out[1] = turned
        sums[1:2, :] = jnp.sum(turned.astype(F32), axis=0, keepdims=True)
        plain = val_sum[...].astype(BF16)
        out[2] = plain
        sums[2:3, :] = jnp.sum(plain.astype(F32), axis=0, keepdims=True)


def attend_back(
    queries, keys, vals, grads, logs, seg_col, seg_row, cosine, sine, first, count, held, start, before=(), block=256
):
    rows = queries.shape[0]
    some = pl.BlockSpec((block, PAIR), lambda p, i: (i, p + first))
    full = pl.BlockSpec((rows, PAIR), lambda p, i: (0, p + first))
    return pl.pallas_call(
        attend_back_body,
        grid=(count, rows // block),
        in_specs=[
            some,
            full,
            full,
            some,
            pl.BlockSpec((None, 8, block), lambda p, i: (p + first, 0, i)),
            whole((rows, 1)),
            pl.BlockSpec((1, block), lambda p, i: (0, i)),
            pl.BlockSpec((block, PAIR), lambda p, i: (i, 0)),
            pl.BlockSpec((block, PAIR), lambda p, i: (i, 0)),
            whole((rows, PAIR)),
            whole((rows, PAIR)),
        ]
        + [pl.BlockSpec(memory_space=pl.ANY)] * len(before),
        out_specs=[
            pl.BlockSpec((3, rows, PAIR), lambda p, i: (0, 0, p + start)),
            pl.BlockSpec((8, PAIR), lambda p, i: (0, p + start)),
        ],
        out_shape=[
            jax.ShapeDtypeStruct((3, rows, held * PAIR), BF16),
            jax.ShapeDtypeStruct((8, held * PAIR), F32),
        ],
        input_output_aliases={11 + at: at for at in range(len(before))},
        scratch_shapes=[pltpu.VMEM((rows, PAIR), F32)] * 2,
        compiler_params=params("arbitrary", "arbitrary"),
        cost_estimate=cost(40 * rows * rows * PAIR * count, 14 * rows * PAIR * count, 2 * rows * rows * count),
        name="attend_back",
    )(queries, keys, vals, grads, logs, seg_col, seg_row, cosine, sine, cosine, sine, *before)


GELU_A = 0.7978845608028654
GELU_B = 0.044715


def feed_body(
    x, own, other, outer_bias, gate_attend, shift, scale, gate_feed, up, up_bias, down, cot, *rest
):
    normed, acted, lift_grad, feed_cot, feed_part, grad_part, sums = rest[-7:]
    attend_sum = own[...] + other[...] + outer_bias[...]
    middle = x[...].astype(F32) + gate_attend[...] * attend_sum
    unit, _ = normalise(middle)
    rounded = (unit * (1.0 + scale[...]) + shift[...]).astype(BF16)
    normed[...] = rounded
    lifted = mm(rounded, up[...]) + up_bias[...]
    square = lifted * lifted
    tanh = jnp.tanh(GELU_A * lifted * (1.0 + GELU_B * square))
    half = 0.5 * (1.0 + tanh)
    active = (lifted * half).astype(BF16)
    slope = half + 0.5 * lifted * (1.0 - tanh * tanh) * (GELU_A * (1.0 + 3.0 * GELU_B * square))
    acted[...] = active
    part = mm(active, down[...])
    feed_part[...] = part
    g = cot[...].astype(F32)
    fc = (gate_feed[...] * g).astype(BF16)
    feed_cot[...] = fc
    lg = (mm(fc, down[...], NT) * slope).astype(BF16)
    lift_grad[...] = lg
    grad_part[...] = mm(lg, up[...], NT)
    sums[...] = jnp.zeros_like(sums)
    sums[0:1, :] = jnp.sum(g * part, axis=0, keepdims=True)
    sums[1:2, :] = jnp.sum(fc.astype(F32), axis=0, keepdims=True)
    sums[2:3, : lg.shape[1]] = jnp.sum(lg.astype(F32), axis=0, keepdims=True)
    sums[3:4, :] = jnp.sum(g, axis=0, keepdims=True)


def feed(x, own, other, outer_bias, gate_attend, shift, scale, gate_feed, up, up_bias, down, cot, before, block=256):
    tok, width = x.shape
    units = up.shape[1]
    blocks = tok // block
    start = 0 if before is None else blocks
    row = pl.BlockSpec((block, width), lambda i: (i, 0))
    at = lambda cols: pl.BlockSpec((block, cols), lambda i: (i + start, 0))
    vec = whole((1, width))
    wide = jax.ShapeDtypeStruct((2 * tok, width), BF16)
    thin = jax.ShapeDtypeStruct((2 * tok, units), BF16)
    part = jax.ShapeDtypeStruct((tok, width), F32)
    before = [] if before is None else before
    return pl.pallas_call(
        feed_body,
        grid=(blocks,),
        in_specs=[
            row, row, row, vec, vec, vec, vec, vec,
            whole(up.shape), whole((1, units)), whole(down.shape), row,
        ] + [pl.BlockSpec(memory_space=pl.ANY)] * len(before),
        out_specs=[
            at(width), at(units), at(units), at(width), row, row,
            pl.BlockSpec((None, 8, width), lambda i: (i, 0, 0)),
        ],
        out_shape=[wide, thin, thin, wide, part, part, jax.ShapeDtypeStruct((blocks, 8, width), F32)],
        input_output_aliases={12 + i: i for i in range(len(before))},
        compiler_params=params("arbitrary"),
        cost_estimate=cost(8 * tok * width * units, 24 * tok * width + 4 * tok * units + 4 * width * units, tok * units),
        name="feed",
    )(x, own, other, outer_bias, gate_attend, shift, scale, gate_feed, up, up_bias, down, cot, *before)


def middle_body(
    x, own, other, outer_bias, gate_attend, scale, grad_own, grad_other, cot, outer, *rest
):
    middle_grad, attend_cot, heads_grad, sums = rest[-4:]
    attend_sum = own[...] + other[...] + outer_bias[...]
    middle = x[...].astype(F32) + gate_attend[...] * attend_sum
    unit, inverse = normalise(middle)
    grad = grad_own[...] + grad_other[...]
    mg = cot[...].astype(F32) + norm_back(grad, unit, inverse, scale[...])
    middle_grad[...] = mg.astype(middle_grad.dtype)
    ac = (gate_attend[...] * mg).astype(BF16)
    attend_cot[...] = ac
    heads_grad[...] = mm(ac, outer[...], NT).astype(BF16)
    sums[...] = jnp.zeros_like(sums)
    sums[0:1, :] = jnp.sum(grad, axis=0, keepdims=True)
    sums[1:2, :] = jnp.sum(grad * unit, axis=0, keepdims=True)
    sums[2:3, :] = jnp.sum(mg * attend_sum, axis=0, keepdims=True)
    sums[3:4, :] = jnp.sum(ac.astype(F32), axis=0, keepdims=True)


def middle_back(x, own, other, outer_bias, gate_attend, scale, grad_own, grad_other, cot, outer, upper, before, block=256):
    tok, width = x.shape
    local = outer.shape[0]
    blocks = tok // block
    start = blocks if upper else 0
    row = pl.BlockSpec((block, width), lambda i: (i, 0))
    at = lambda cols: pl.BlockSpec((block, cols), lambda i: (i + start, 0))
    vec = whole((1, width))
    return pl.pallas_call(
        middle_body,
        grid=(blocks,),
        in_specs=[row, row, row, vec, vec, vec, row, row, row, whole(outer.shape)]
        + [pl.BlockSpec(memory_space=pl.ANY)] * len(before),
        out_specs=[row, at(width), at(local), pl.BlockSpec((None, 8, width), lambda i: (i, 0, 0))],
        out_shape=[
            jax.ShapeDtypeStruct((tok, width), F32),
            jax.ShapeDtypeStruct((2 * tok, width), BF16),
            jax.ShapeDtypeStruct((2 * tok, local), BF16),
            jax.ShapeDtypeStruct((blocks, 8, width), F32),
        ],
        input_output_aliases={10 + i: 1 + i for i in range(len(before))},
        compiler_params=params("arbitrary"),
        cost_estimate=cost(2 * tok * width * local, 26 * tok * width),
        name="middle_back",
    )(x, own, other, outer_bias, gate_attend, scale, grad_own, grad_other, cot, outer, *before)


def spread_body(*refs):
    parts, weight, out = refs[:-2], refs[-2], refs[-1]
    total = None
    for j in range(3):
        grads = jnp.concatenate([part[j] for part in parts], axis=1)
        grown = mm(grads, weight[j], NT)
        total = grown if total is None else total + grown
    out[...] = total


def spread(parts, weight, first, count, block=256):
    local = weight.shape[2]
    width = weight.shape[1]
    some = lambda part: pl.BlockSpec((3, block, part.shape[2]), lambda i: (0, i + first // block, 0))
    return pl.pallas_call(
        spread_body,
        grid=(count // block,),
        in_specs=[some(part) for part in parts] + [whole(weight.shape)],
        out_specs=pl.BlockSpec((block, width), lambda i: (i, 0)),
        out_shape=jax.ShapeDtypeStruct((count, width), F32),
        compiler_params=params("arbitrary"),
        cost_estimate=cost(6 * count * local * width, 6 * (count * local + local * width) + 4 * count * width),
        name="spread",
    )(*parts, weight)


def final_body(x, scale, own, other, middle_grad, frames_grad, sums):
    unit, inverse = normalise(x[...].astype(F32))
    grad = own[...] + other[...]
    frames_grad[...] = middle_grad[...] + norm_back(grad, unit, inverse, scale[...])
    sums[...] = jnp.zeros_like(sums)
    sums[0:1, :] = jnp.sum(grad, axis=0, keepdims=True)
    sums[1:2, :] = jnp.sum(grad * unit, axis=0, keepdims=True)


def final_back(x, scale, own, other, middle_grad):
    rows, width = x.shape
    block = min(256, rows)
    blocks = rows // block
    row = pl.BlockSpec((block, width), lambda i: (i, 0))
    return pl.pallas_call(
        final_body,
        grid=(blocks,),
        in_specs=[row, whole((1, width)), row, row, row],
        out_specs=[row, pl.BlockSpec((None, 8, width), lambda i: (i, 0, 0))],
        out_shape=[jax.ShapeDtypeStruct((rows, width), F32), jax.ShapeDtypeStruct((blocks, 8, width), F32)],
        compiler_params=params("arbitrary"),
        cost_estimate=cost(20 * rows * width, 16 * rows * width),
        name="final_back",
    )(x, scale, own, other, middle_grad)


def cross(values, mask):
    return lax.ppermute(values, "dp", [(i, i ^ mask) for i in range(16)])


def crossed(sends):
    return [cross(values, mask) for values, mask in sends]


class Reduce:
    def __init__(self, values, index):
        self.index = index
        cols = values[0].shape[-1]
        self.values = [v.reshape(-1, 4, 4, v.shape[-2] // 16, cols) for v in values]
        self.rows = self.values[0].shape[3] // 2

    def take(self, mask):
        at = (self.index % 4) ^ mask
        return [lax.dynamic_index_in_dim(v, at, 2, keepdims=False) for v in self.values]

    def first(self):
        far, rows = self.take(3), self.rows
        pack = lambda part: jnp.concatenate([f[:, :, part].astype(BF16) for f in far], axis=0)
        return [(pack(slice(0, rows)), 1), (pack(slice(rows, None)), 2)]

    def second(self, got):
        rows = self.rows
        joined = lambda mask: jnp.concatenate(self.take(mask), axis=0)
        to_x, to_y = joined(1), joined(2)
        none = jnp.zeros_like(got[0])
        to_x = (to_x + jnp.concatenate([none, got[1]], axis=2).astype(F32)).astype(BF16)
        to_y = (to_y + jnp.concatenate([got[0], none], axis=2).astype(F32)).astype(BF16)
        return [(to_x, 1), (to_y, 2)]

    def third(self, got):
        self.near = jnp.concatenate(self.take(0), axis=0) + (got[0].astype(F32) + got[1].astype(F32))
        at = self.index // 4
        block = lambda mask: lax.dynamic_index_in_dim(self.near, at ^ mask, 1, keepdims=False)
        self.own = block(0)
        return [(block(mask).astype(BF16), 4 * mask) for mask in (1, 2, 3)]

    def last(self, got):
        got = [g.astype(F32) for g in got]
        return ((self.own + got[0]) + (got[1] + got[2])).astype(BF16)


def cut_columns(values, cols):
    return jnp.concatenate([values[..., at : at + cols] for at in range(0, values.shape[-1], cols)], axis=0)


def joined(sends, more):
    return [(jnp.concatenate([values, more], axis=0), mask) for values, mask in sends]


def split(got, count):
    return [g[:count] for g in got], [g[count:] for g in got]


class Spread:
    def __init__(self, own):
        self.own = own

    def first(self):
        return [(self.own, 1), (self.own, 2)]

    def second(self, got):
        self.side = got
        rows = self.own.shape[2] // 2
        return [(got[1][:, :, :rows], 1), (got[0][:, :, rows:], 2)]

    def parts(self, got):
        return (self.own, *self.side, *got)


def placed(index, refs):
    own, side_x, side_y, far_low, far_high = refs
    rows = own.shape[1]
    half = rows // 2
    here = index[0] % 4
    return [
        (here, slice(0, rows), own),
        (here ^ 1, slice(0, rows), side_x),
        (here ^ 2, slice(0, rows), side_y),
        (here ^ 3, slice(0, half), far_low),
        (here ^ 3, slice(half, rows), far_high),
    ]


def assemble_heads_body(index, *refs):
    inner, outer = refs[5:]
    cols = refs[0].shape[2]
    for at, span, ref in placed(index, refs[:5]):
        inner[:, at, span, :cols] = ref[0:3].astype(F32)
        inner[:, at, span, cols:] = ref[5:8].astype(F32)
        outer[at, span, :cols] = ref[3].astype(F32)
        outer[at, span, cols:] = ref[4].astype(F32)


def assemble_feed_body(index, *refs):
    cols = refs[0].shape[2]
    for at, span, ref in placed(index, refs[:5]):
        for part in range(8):
            refs[5 + part % 2][at, span, (part // 2) * cols : (part // 2 + 1) * cols] = ref[part].astype(F32)


def assemble(body, index, parts, out_specs, out_shape):
    _, count, rows, cols = parts[0].shape
    spec = lambda r: pl.BlockSpec(
        (None, count, r, cols), lambda z, index: (z ^ (index[0] // 4), 0, 0, 0)
    )
    return pl.pallas_call(
        body,
        grid_spec=pltpu.PrefetchScalarGridSpec(
            num_scalar_prefetch=1,
            grid=(4,),
            in_specs=[spec(rows)] * 3 + [spec(rows // 2)] * 2,
            out_specs=out_specs,
        ),
        out_shape=[jax.ShapeDtypeStruct(shape, F32) for shape in out_shape],
        compiler_params=params("arbitrary"),
        cost_estimate=cost(0, 6 * count * 16 * rows * cols),
        name="assemble",
    )(index[None], *parts)


def assemble_heads(index, *parts):
    _, count, rows, cols = parts[0].shape
    inner, outer = assemble(
        assemble_heads_body, index, parts,
        [
            pl.BlockSpec((3, 4, rows, 2 * cols), lambda z, index: (0, z, 0, 0)),
            pl.BlockSpec((4, rows, 2 * cols), lambda z, index: (z % 2, 0, z // 2)),
        ],
        [(3, 16, rows, 2 * cols), (8, rows, 4 * cols)],
    )
    return inner.reshape(3, 16 * rows, 2 * cols), outer.reshape(8 * rows, 4 * cols)


def assemble_feed(index, *parts):
    _, count, rows, cols = parts[0].shape
    outs = assemble(
        assemble_feed_body, index, parts,
        [pl.BlockSpec((4, rows, 4 * cols), lambda z, index: (z, 0, 0))] * 2,
        [(16, rows, 4 * cols)] * 2,
    )
    return [out.reshape(16 * rows, 4 * cols) for out in outs]


def tie(*groups):
    leaves, tree = jax.tree.flatten(groups)
    held = iter(lax.optimization_barrier(tuple(v for v in leaves if hasattr(v, "dtype"))))
    return jax.tree.unflatten(tree, [next(held) if hasattr(v, "dtype") else v for v in leaves])


def fold(parts):
    while parts.shape[0] > 1:
        parts = parts[0::2] + parts[1::2]
    return parts[0]


def tables(lengths, row_len, offset):
    frame_index = (jnp.arange(row_len, dtype=jnp.int32) + offset) % row_len
    seg_ends = jnp.cumsum(lengths)
    segment = jnp.sum((frame_index[:, None] >= seg_ends[None, :]).astype(jnp.int32), axis=1)
    starts = seg_ends - lengths
    picked = jnp.arange(lengths.shape[0], dtype=jnp.int32)[None, :] == segment[:, None]
    before = jnp.sum(jnp.where(picked, starts[None, :], 0), axis=1)
    position = (frame_index - before).astype(F32)
    half = HEAD_DIM // 2
    lane = jnp.arange(PAIR, dtype=jnp.int32)
    frequency = 10000.0 ** (-(lane % half).astype(F32) / half)
    sign = jnp.where(lane % HEAD_DIM < half, -1.0, 1.0).astype(F32)
    angles = position[:, None] * frequency[None, :]
    return segment, jnp.cos(angles), jnp.sin(angles) * sign[None, :]


def per_device(
    frames, time_embed, seg_lengths, mod_weight, mod_bias, inner_weight, inner_bias, outer_weight,
    outer_bias, up_weight, up_bias, down_weight, down_bias, cotangent,
):
    own_tok, width = frames.shape
    group = lax.axis_size("tensor")
    size = lax.axis_size("dp")
    index = lax.axis_index("dp")
    rank = lax.axis_index("tensor")
    rows = own_tok * group
    tok = rows // 2
    paired = group == 2
    staged = size == 16
    pairs = inner_weight.shape[2] // PAIR
    swap = lambda v: lax.ppermute(v, "tensor", [(0, 1), (1, 0)])

    def halves(values):
        if paired:
            return values, swap(values)
        full = lax.all_gather(values, "tensor", axis=0, tiled=True)
        return full[:tok], full[tok:]

    def summed(low, high):
        if paired:
            other_low, other_high = swap(high), swap(low)
            return (low, other_low), (high, other_high)
        low, high = lax.psum((low, high), "tensor")
        none = jnp.zeros_like(low)
        return (low, none), (high, none)

    def own_rows(low, high):
        full = jnp.concatenate([low, high], axis=0)
        return lax.dynamic_slice_in_dim(full, rank * own_tok, own_tok, 0)

    def tensor_sum(values):
        return values + swap(values) if paired else lax.psum(values, "tensor")

    x_low, x_high = halves(frames)
    cot_low, cot_high = halves(cotangent)
    segment, cosine, sine = tables(seg_lengths[0], rows, rank * tok if paired else 0)
    seg_col, seg_row = segment[:, None], segment[None, :]
    acted = jax.nn.silu(time_embed.astype(F32)).astype(BF16)
    mod_part = jnp.dot(acted, mod_weight, preferred_element_type=F32) + mod_bias.astype(F32)
    if paired:
        other = swap(mod_part)
        first = rank == 0
        modulation = jnp.concatenate(
            [jnp.where(first, mod_part, other), jnp.where(first, other, mod_part)], axis=1
        )
    else:
        modulation = lax.all_gather(mod_part, "tensor", axis=1, tiled=True)
    shift_attend, scale_attend, gate_attend, shift_feed, scale_feed, gate_feed = [
        modulation[:, column * width : (column + 1) * width] for column in range(6)
    ]
    normed, queries, keys, vals = project(
        x_low, x_high, shift_attend, scale_attend, inner_weight, inner_bias.astype(F32), cosine, sine
    )
    mixed, logs, part_low, part_high = attend(queries, keys, vals, seg_col, seg_row, outer_weight)
    (own_low, other_low), (own_high, other_high) = summed(part_low, part_high)
    outer_vec = outer_bias.astype(F32)[None, :]
    feed_rest = (
        outer_vec, gate_attend, shift_feed, scale_feed, gate_feed,
        up_weight, up_bias.astype(F32)[None, :], down_weight,
    )
    *shared, feed_low, grad_low, sums_low = feed(
        x_low, own_low, other_low, *feed_rest, cot_low, None
    )
    *shared, feed_high, grad_high, sums_high = feed(
        x_high, own_high, other_high, *feed_rest, cot_high, shared
    )
    normed_feed, active, lift_grad, feed_cot = shared
    feed_vec = fold(jnp.concatenate([sums_low, sums_high]))
    (grad_low, grad_low_other), (grad_high, grad_high_other) = summed(grad_low, grad_high)
    down_grad = mm(active, feed_cot, TN)
    up_grad = mm(normed_feed, lift_grad, TN)
    middle_rest = (outer_vec, gate_attend, scale_feed)

    if staged:
        one = Reduce([down_grad, up_grad], index)
        sends = one.first()
        grad_low_other, sends = tie(grad_low_other, sends)
        got = crossed(sends)
    middle_high, *shared, vec_high = middle_back(
        x_high, own_high, other_high, *middle_rest, grad_high, grad_high_other, cot_high,
        outer_weight, True, [],
    )
    middle_low, attend_cot, heads_grad, vec_low = middle_back(
        x_low, own_low, other_low, *middle_rest, grad_low, grad_low_other, cot_low,
        outer_weight, False, shared,
    )
    if staged:
        middle_low, attend_cot, heads_grad, vec_low, vec_high, got = tie(
            middle_low, attend_cot, heads_grad, vec_low, vec_high, got
        )
        sends = one.second(got)
    middle_vec = fold(jnp.concatenate([vec_low, vec_high]))
    outer_grad = mm(mixed, attend_cot, TN)

    back = lambda grads, *where: attend_back(
        queries, keys, vals, grads, logs, seg_col, seg_row, cosine, sine, *where
    )
    inner_grad = lambda part: [mm(normed, part[j], TN) for j in range(3)]
    if staged:
        early = pairs // 2
        heads_grad, sends = tie(heads_grad, sends)
        got = crossed(sends)
        near = back(heads_grad, 0, early, early, 0)
        near, got = tie(near, got)
        sends = one.third(got)
        cols = [outer_grad[:, at : at + early * PAIR] for at in range(0, width, early * PAIR)]
        cols = [jnp.concatenate([cols[at], cols[at + 2]], axis=0) for at in (0, 1)]
        two = Reduce(inner_grad(near[0]) + cols, index)
        sends2 = two.first()
        heads_grad, sends, sends2 = tie(heads_grad, sends, sends2)
        got, got2 = crossed(sends), crossed(sends2)
        late = pairs - early
        far = back(heads_grad, early, late // 2, late, 0)
        far, got2, got[1] = tie(far, got2, got[1])
        sends2 = two.second(got2)
        heads_grad, sends2 = tie(heads_grad, sends2)
        got2 = crossed(sends2)
        far = back(heads_grad, early + late // 2, late - late // 2, late, late // 2, far)
        far, got, got2 = tie(far, got, got2)
        mine1 = cut_columns(one.last(got), early * PAIR)
        sends2 = joined(two.third(got2), mine1)
        three = Reduce(inner_grad(far[0]), index)
        sends3 = three.first()
        results = [near, far]
    else:
        results = [back(heads_grad, 0, pairs, pairs, 0)]
        inner_grads = inner_grad(results[0][0])
    parts = [part for part, _ in results]
    part_sums = jnp.concatenate([sums for _, sums in results], axis=1)

    if staged:
        parts[-1], sends2, sends3, feed_low, feed_high = tie(
            parts[-1], sends2, sends3, feed_low, feed_high
        )
        got3, got2 = crossed(sends3), crossed(sends2)
    if paired:
        spread_other = spread(parts, inner_weight, tok, tok)
        if staged:
            spread_other, got3 = tie(spread_other, got3)
            sends3 = three.second(got3)
            parts[-1], sends3 = tie(parts[-1], sends3)
            got3 = crossed(sends3)
        spread_other = swap(spread_other)
        spread_own = spread(parts, inner_weight, 0, tok)
        own_middle = middle_low
    else:
        both = lax.psum(spread(parts, inner_weight, 0, rows), "tensor")
        spread_own = own_rows(both[:tok], both[tok:])
        spread_other = jnp.zeros_like(spread_own)
        own_middle = own_rows(middle_low, middle_high)
    if staged:
        spread_own, got2, got3 = tie(spread_own, got2, got3)
        got2, got1 = split(got2, two.own.shape[0])
        mine2 = two.last(got2)
        feed_grads = Spread(jnp.stack([mine1] + got1))
        sends1 = feed_grads.first()
        sends3 = joined(three.third(got3), mine2)
        spread_own, sends1, sends3, feed_low = tie(spread_own, sends1, sends3, feed_low)
        got3, got1 = crossed(sends3), crossed(sends1)
    frames_grad, final_sums = final_back(frames, scale_attend, spread_own, spread_other, own_middle)
    if staged:
        frames_grad, final_sums, got3 = tie(frames_grad, final_sums, got3)
        got3, got2 = split(got3, three.own.shape[0])
        mine3 = three.last(got3)
        _, got1 = tie(mine3, got1)
        got3 = crossed([(mine3, 4 * mask) for mask in (1, 2, 3)])

    if paired:
        feed_sum = feed_low + swap(feed_high)
        attend_sum = own_low + other_low + outer_vec
    else:
        feed_sum = own_rows(*lax.psum((feed_low, feed_high), "tensor"))
        attend_sum = own_rows(own_low, own_high) + outer_vec
    feed_sum = feed_sum + down_bias.astype(F32)[None, :]
    output = (frames.astype(F32) + gate_attend * attend_sum + gate_feed * feed_sum).astype(BF16)

    final_vec = fold(final_sums)

    crossing = tensor_sum(jnp.concatenate([final_vec[0:1], final_vec[1:2], feed_vec[0:1]], axis=1))
    gate_feed_grad = crossing[:, 2 * width :] + down_bias.astype(F32)[None, :] * feed_vec[3:4]
    mod_full = jnp.concatenate(
        [crossing[:, : 2 * width], middle_vec[2:3], middle_vec[0:1], middle_vec[1:2], gate_feed_grad],
        axis=1,
    )
    share = mod_weight.shape[1]
    local = inner_weight.shape[2]
    units = up_weight.shape[1]
    mod_grad = lax.dynamic_slice_in_dim(mod_full, rank * share, share, 1).astype(BF16)
    inner_biases = [part_sums[j] for j in range(3)]
    biases = jnp.concatenate(inner_biases + [feed_vec[2, :units], middle_vec[3], feed_vec[1]])
    small = jnp.concatenate([acted.astype(F32), mod_grad.astype(F32), biases[None, :]], axis=1)
    if staged:
        near = jnp.concatenate([small] + [cross(small, mask) for mask in (1, 2, 3)], axis=0)
        small = jnp.concatenate([near] + [cross(near, 4 * mask) for mask in (1, 2, 3)], axis=0)
        slot = jnp.arange(size, dtype=jnp.int32)
        order = ((slot[:, None] ^ index) == slot[None, :]).astype(BF16)
        factors = mm(order, small[:, : width + share].astype(BF16)).astype(BF16)
        biases = fold(small[:, width + share :][:, None, :])[0]
    else:
        small = lax.all_gather(small, "dp", axis=0, tiled=True)
        factors = small[:, : width + share].astype(BF16)
        biases = jnp.sum(small[:, width + share :], axis=0)
    all_acted, all_mod = factors[:, :width], factors[:, width:]
    mod_weight_grad = mm(all_acted, all_mod, TN)
    mod_bias_grad = jnp.sum(all_mod.astype(F32), axis=0)
    acted_grad = tensor_sum(mm(mod_grad, mod_weight, NT))
    time_grad = jax.vjp(jax.nn.silu, time_embed.astype(F32))[1](acted_grad)[0]

    if staged:
        got1 = crossed(feed_grads.second(got1))
        both = lambda a, b: jnp.concatenate([a, b], axis=0)
        head_grads = Spread(jnp.stack([both(mine2, mine3)] + [both(a, b) for a, b in zip(got2, got3)]))
        sends = head_grads.first()
        _, got1 = tie(sends, got1)
        got = crossed(sends)
        down_total, up_total = assemble_feed(index, *feed_grads.parts(got1))
        got = crossed(head_grads.second(got))
        inner_total, outer_total = assemble_heads(index, *head_grads.parts(got))
    else:
        inner_total = jnp.stack(inner_grads)
        down_total, up_total, outer_total, inner_total = lax.psum(
            (down_grad, up_grad, outer_grad, inner_total), "dp"
        )

    cut = 3 * local
    return (
        output,
        frames_grad,
        time_grad,
        mod_weight_grad,
        mod_bias_grad,
        inner_total,
        biases[:cut].reshape(3, local),
        outer_total,
        biases[cut + units : cut + units + width],
        up_total,
        biases[cut : cut + units],
        down_total,
        biases[cut + units + width :],
    )


def solution(mesh):
    in_specs = (
        P(("dp", "tensor"), None),
        P("dp", None),
        P("dp", None),
        P(None, "tensor"),
        P("tensor"),
        P(None, None, "tensor"),
        P(None, "tensor"),
        P("tensor", None),
        P(),
        P(None, "tensor"),
        P("tensor"),
        P("tensor", None),
        P(),
        P(("dp", "tensor"), None),
    )
    out_specs = (
        P(("dp", "tensor"), None),
        P(("dp", "tensor"), None),
        P("dp", None),
        P(None, "tensor"),
        P("tensor"),
        P(None, None, "tensor"),
        P(None, "tensor"),
        P("tensor", None),
        P(),
        P(None, "tensor"),
        P("tensor"),
        P("tensor", None),
        P(),
    )
    return jax.shard_map(
        per_device, mesh=mesh, in_specs=in_specs, out_specs=out_specs, check_vma=False
    )
```

```python
import functools

import jax
import jax.numpy as jnp
from jax import lax
from jax.experimental import pallas as pl
from jax.experimental.pallas import tpu as pltpu
from jax.sharding import PartitionSpec as P

HEAD_DIM = 64
PAIR = 2 * HEAD_DIM
EPS = 1e-06
F32 = jnp.float32
BF16 = jnp.bfloat16
NT = (((1,), (1,)), ((), ()))
TN = (((0,), (0,)), ((), ()))
COST_SCALE = 1000
VMEM_LIMIT = 56 * 1024 * 1024


def mm(a, b, dims=(((1,), (0,)), ((), ()))):
    return lax.dot_general(a, b, dims, preferred_element_type=F32)


def normalise(values):
    centred = values - jnp.mean(values, axis=-1, keepdims=True)
    inverse = lax.rsqrt(jnp.mean(centred * centred, axis=-1, keepdims=True) + EPS)
    return centred * inverse, inverse


def norm_back(grad, unit, inverse, scale):
    lifted = grad * (1.0 + scale)
    mean_one = jnp.mean(lifted, axis=-1, keepdims=True)
    mean_two = jnp.mean(lifted * unit, axis=-1, keepdims=True)
    return inverse * (lifted - mean_one - unit * mean_two)


def swap_halves(values):
    width = values.shape[-1]
    lane = lax.broadcasted_iota(jnp.int32, values.shape, 1)
    ahead = pltpu.roll(values, width - HEAD_DIM // 2, 1)
    behind = pltpu.roll(values, HEAD_DIM // 2, 1)
    return jnp.where(lane % HEAD_DIM < HEAD_DIM // 2, ahead, behind)


def head_mask(which, dtype):
    lane = lax.broadcasted_iota(jnp.int32, (1, PAIR), 1)
    return jnp.where(lane // HEAD_DIM == which, 1.0, 0.0).astype(dtype)


def whole(shape):
    return pl.BlockSpec(shape, lambda *_: (0,) * len(shape))


def params(*semantics):
    return pltpu.CompilerParams(dimension_semantics=semantics, vmem_limit_bytes=VMEM_LIMIT)


def cost(flops, bytes_accessed, transcendentals=0):
    return pl.CostEstimate(
        flops=int(flops // COST_SCALE), bytes_accessed=int(bytes_accessed // COST_SCALE), transcendentals=0
    )


def pick(step, half, low, high):
    return jnp.where(step < half, low, high)


def low_map(half):
    return lambda i, *_: (jnp.minimum(i, half - 1), 0)


def high_map(half):
    return lambda i, *_: (jnp.maximum(i - half, 0), 0)


def project_body(low, high, shift, scale, weight, bias, cosine, sine, normed, queries, keys, vals):
    x = pick(pl.program_id(0), pl.num_programs(0) // 2, low[...], high[...])
    unit, _ = normalise(x.astype(F32))
    rounded = (unit * (1.0 + scale[...]) + shift[...]).astype(BF16)
    normed[...] = rounded
    repeats = weight.shape[2] // PAIR
    cos = jnp.concatenate([cosine[...]] * repeats, axis=1)
    sin = jnp.concatenate([sine[...]] * repeats, axis=1)
    first = mm(rounded, weight[0]) + bias[0:1, :]
    queries[...] = ((first * cos + swap_halves(first) * sin) * HEAD_DIM ** (-0.5)).astype(BF16)
    second = mm(rounded, weight[1]) + bias[1:2, :]
    keys[...] = (second * cos + swap_halves(second) * sin).astype(BF16)
    vals[...] = (mm(rounded, weight[2]) + bias[2:3, :]).astype(BF16)


def project(low, high, shift, scale, weight, bias, cosine, sine, block=256):
    rows, width = 2 * low.shape[0], low.shape[1]
    local = weight.shape[2]
    half = rows // block // 2
    row = lambda cols: pl.BlockSpec((block, cols), lambda i: (i, 0))
    return pl.pallas_call(
        project_body,
        grid=(rows // block,),
        in_specs=[
            pl.BlockSpec((block, width), low_map(half)),
            pl.BlockSpec((block, width), high_map(half)),
            whole((1, width)),
            whole((1, width)),
            whole(weight.shape),
            whole(bias.shape),
            row(PAIR),
            row(PAIR),
        ],
        out_specs=[row(width), row(local), row(local), row(local)],
        out_shape=[jax.ShapeDtypeStruct((rows, width), BF16)]
        + [jax.ShapeDtypeStruct((rows, local), BF16)] * 3,
        compiler_params=params("arbitrary"),
        cost_estimate=cost(6 * rows * width * local, 4 * rows * width + 6 * rows * local + 6 * width * local),
        name="project",
    )(low, high, shift, scale, weight, bias, cosine, sine)


def attend_body(queries, keys, vals, seg_col, seg_row, outer, mixed, logs, low, high):
    step, pair = pl.program_id(0), pl.program_id(1)
    half = pl.num_programs(0) // 2
    q, k, v = queries[...], keys[...], vals[...]
    allowed = seg_col[...] == seg_row[...]
    total = None
    for which in (0, 1):
        raw = mm(q * head_mask(which, BF16), k, NT)
        raw = jnp.where(allowed, raw, -1e30)
        largest = jnp.max(raw, axis=-1, keepdims=True)
        powers = jnp.exp(raw - largest)
        sums = jnp.sum(powers, axis=-1, keepdims=True)
        weights = (powers * (1.0 / sums)).astype(BF16)
        part = mm(weights, v) * head_mask(which, F32)
        total = part if total is None else total + part
        stat = jnp.broadcast_to(largest + jnp.log(sums), (q.shape[0], PAIR))
        logs[which : which + 1, :] = jnp.transpose(stat)[0:1, :]
    rounded = total.astype(BF16)
    mixed[...] = rounded
    grown = mm(rounded, outer[...])
    for ref, here in ((low, step < half), (high, step >= half)):

        @pl.when(jnp.logical_and(here, pair == 0))
        def _(ref=ref):
            ref[...] = grown

        @pl.when(jnp.logical_and(here, pair > 0))
        def _(ref=ref):
            ref[...] += grown


def attend(queries, keys, vals, seg_col, seg_row, outer, block=512):
    rows, local = queries.shape
    width = outer.shape[1]
    pairs = local // PAIR
    half = rows // block // 2
    part = jax.ShapeDtypeStruct((rows // 2, width), F32)
    return pl.pallas_call(
        attend_body,
        grid=(rows // block, pairs),
        in_specs=[
            pl.BlockSpec((block, PAIR), lambda i, p: (i, p)),
            pl.BlockSpec((rows, PAIR), lambda i, p: (0, p)),
            pl.BlockSpec((rows, PAIR), lambda i, p: (0, p)),
            pl.BlockSpec((block, 1), lambda i, p: (i, 0)),
            whole((1, rows)),
            pl.BlockSpec((PAIR, width), lambda i, p: (p, 0)),
        ],
        out_specs=[
            pl.BlockSpec((block, PAIR), lambda i, p: (i, p)),
            pl.BlockSpec((None, 8, block), lambda i, p: (p, 0, i)),
            pl.BlockSpec((block, width), low_map(half)),
            pl.BlockSpec((block, width), high_map(half)),
        ],
        out_shape=[
            jax.ShapeDtypeStruct((rows, local), BF16),
            jax.ShapeDtypeStruct((pairs, 8, rows), F32),
            part,
            part,
        ],
        compiler_params=params("arbitrary", "arbitrary"),
        cost_estimate=cost(20 * rows * rows * local, 8 * rows * local, 2 * pairs * rows * rows),
        name="attend",
    )(queries, keys, vals, seg_col, seg_row, outer)


def attend_back_body(
    queries, keys, vals, grads, logs, seg_col, seg_row, cos_q, sin_q, cos_k, sin_k, *rest
):
    out, sums, key_sum, val_sum = rest[-4:]
    step = pl.program_id(1)
    block = queries.shape[0]
    q, k, v, g = queries[...], keys[...], vals[...], grads[...]

    @pl.when(step == 0)
    def _():
        key_sum[...] = jnp.zeros_like(key_sum)
        val_sum[...] = jnp.zeros_like(val_sum)
        sums[...] = jnp.zeros_like(sums)

    allowed = seg_col[...] == seg_row[...]
    total = None
    for which in (0, 1):
        qh = q * head_mask(which, BF16)
        gh = g * head_mask(which, BF16)
        raw = jnp.where(allowed, mm(k, qh, NT), -1e30)
        probs = jnp.exp(raw - logs[which : which + 1, :])
        prob_grad = mm(v, gh, NT)
        centre = jnp.sum(probs * prob_grad, axis=0, keepdims=True)
        score = (probs * (prob_grad - centre)).astype(BF16)
        val_sum[...] += mm(probs.astype(BF16), gh)
        key_sum[...] += mm(score, qh)
        part = mm(score, k, TN) * head_mask(which, F32)
        total = part if total is None else total + part
    total = total * HEAD_DIM ** (-0.5)
    turned = (total * cos_q[...] - swap_halves(total) * sin_q[...]).astype(BF16)
    out[0, pl.ds(pl.multiple_of(step * block, block), block), :] = turned
    sums[0:1, :] += jnp.sum(turned.astype(F32), axis=0, keepdims=True)

    @pl.when(step == pl.num_programs(1) - 1)
    def _():
        total = key_sum[...]
        turned = (total * cos_k[...] - swap_halves(total) * sin_k[...]).astype(BF16)
        out[1] = turned
        sums[1:2, :] = jnp.sum(turned.astype(F32), axis=0, keepdims=True)
        plain = val_sum[...].astype(BF16)
        out[2] = plain
        sums[2:3, :] = jnp.sum(plain.astype(F32), axis=0, keepdims=True)


def attend_back(
    queries, keys, vals, grads, logs, seg_col, seg_row, cosine, sine, first, count, held, start, before=(), block=256
):
    rows = queries.shape[0]
    some = pl.BlockSpec((block, PAIR), lambda p, i: (i, p + first))
    full = pl.BlockSpec((rows, PAIR), lambda p, i: (0, p + first))
    return pl.pallas_call(
        attend_back_body,
        grid=(count, rows // block),
        in_specs=[
            some,
            full,
            full,
            some,
            pl.BlockSpec((None, 8, block), lambda p, i: (p + first, 0, i)),
            whole((rows, 1)),
            pl.BlockSpec((1, block), lambda p, i: (0, i)),
            pl.BlockSpec((block, PAIR), lambda p, i: (i, 0)),
            pl.BlockSpec((block, PAIR), lambda p, i: (i, 0)),
            whole((rows, PAIR)),
            whole((rows, PAIR)),
        ]
        + [pl.BlockSpec(memory_space=pl.ANY)] * len(before),
        out_specs=[
            pl.BlockSpec((3, rows, PAIR), lambda p, i: (0, 0, p + start)),
            pl.BlockSpec((8, PAIR), lambda p, i: (0, p + start)),
        ],
        out_shape=[
            jax.ShapeDtypeStruct((3, rows, held * PAIR), BF16),
            jax.ShapeDtypeStruct((8, held * PAIR), F32),
        ],
        input_output_aliases={11 + at: at for at in range(len(before))},
        scratch_shapes=[pltpu.VMEM((rows, PAIR), F32)] * 2,
        compiler_params=params("arbitrary", "arbitrary"),
        cost_estimate=cost(40 * rows * rows * PAIR * count, 14 * rows * PAIR * count, 2 * rows * rows * count),
        name="attend_back",
    )(queries, keys, vals, grads, logs, seg_col, seg_row, cosine, sine, cosine, sine, *before)


GELU_A = 0.7978845608028654
GELU_B = 0.044715


def feed_body(
    x, own, other, outer_bias, gate_attend, shift, scale, gate_feed, up, up_bias, down, cot, *rest
):
    normed, acted, lift_grad, feed_cot, feed_part, grad_part, sums = rest[-7:]
    attend_sum = own[...] + other[...] + outer_bias[...]
    middle = x[...].astype(F32) + gate_attend[...] * attend_sum
    unit, _ = normalise(middle)
    rounded = (unit * (1.0 + scale[...]) + shift[...]).astype(BF16)
    normed[...] = rounded
    lifted = mm(rounded, up[...]) + up_bias[...]
    square = lifted * lifted
    tanh = jnp.tanh(GELU_A * lifted * (1.0 + GELU_B * square))
    half = 0.5 * (1.0 + tanh)
    active = (lifted * half).astype(BF16)
    slope = half + 0.5 * lifted * (1.0 - tanh * tanh) * (GELU_A * (1.0 + 3.0 * GELU_B * square))
    acted[...] = active
    part = mm(active, down[...])
    feed_part[...] = part
    g = cot[...].astype(F32)
    fc = (gate_feed[...] * g).astype(BF16)
    feed_cot[...] = fc
    lg = (mm(fc, down[...], NT) * slope).astype(BF16)
    lift_grad[...] = lg
    grad_part[...] = mm(lg, up[...], NT)
    sums[...] = jnp.zeros_like(sums)
    sums[0:1, :] = jnp.sum(g * part, axis=0, keepdims=True)
    sums[1:2, :] = jnp.sum(fc.astype(F32), axis=0, keepdims=True)
    sums[2:3, : lg.shape[1]] = jnp.sum(lg.astype(F32), axis=0, keepdims=True)
    sums[3:4, :] = jnp.sum(g, axis=0, keepdims=True)


def feed(x, own, other, outer_bias, gate_attend, shift, scale, gate_feed, up, up_bias, down, cot, before, block=256):
    tok, width = x.shape
    units = up.shape[1]
    blocks = tok // block
    start = 0 if before is None else blocks
    row = pl.BlockSpec((block, width), lambda i: (i, 0))
    at = lambda cols: pl.BlockSpec((block, cols), lambda i: (i + start, 0))
    vec = whole((1, width))
    wide = jax.ShapeDtypeStruct((2 * tok, width), BF16)
    thin = jax.ShapeDtypeStruct((2 * tok, units), BF16)
    part = jax.ShapeDtypeStruct((tok, width), F32)
    before = [] if before is None else before
    return pl.pallas_call(
        feed_body,
        grid=(blocks,),
        in_specs=[
            row, row, row, vec, vec, vec, vec, vec,
            whole(up.shape), whole((1, units)), whole(down.shape), row,
        ] + [pl.BlockSpec(memory_space=pl.ANY)] * len(before),
        out_specs=[
            at(width), at(units), at(units), at(width), row, row,
            pl.BlockSpec((None, 8, width), lambda i: (i, 0, 0)),
        ],
        out_shape=[wide, thin, thin, wide, part, part, jax.ShapeDtypeStruct((blocks, 8, width), F32)],
        input_output_aliases={12 + i: i for i in range(len(before))},
        compiler_params=params("arbitrary"),
        cost_estimate=cost(8 * tok * width * units, 24 * tok * width + 4 * tok * units + 4 * width * units, tok * units),
        name="feed",
    )(x, own, other, outer_bias, gate_attend, shift, scale, gate_feed, up, up_bias, down, cot, *before)


def middle_body(
    x, own, other, outer_bias, gate_attend, scale, grad_own, grad_other, cot, outer, *rest
):
    middle_grad, attend_cot, heads_grad, sums = rest[-4:]
    attend_sum = own[...] + other[...] + outer_bias[...]
    middle = x[...].astype(F32) + gate_attend[...] * attend_sum
    unit, inverse = normalise(middle)
    grad = grad_own[...] + grad_other[...]
    mg = cot[...].astype(F32) + norm_back(grad, unit, inverse, scale[...])
    middle_grad[...] = mg.astype(middle_grad.dtype)
    ac = (gate_attend[...] * mg).astype(BF16)
    attend_cot[...] = ac
    heads_grad[...] = mm(ac, outer[...], NT).astype(BF16)
    sums[...] = jnp.zeros_like(sums)
    sums[0:1, :] = jnp.sum(grad, axis=0, keepdims=True)
    sums[1:2, :] = jnp.sum(grad * unit, axis=0, keepdims=True)
    sums[2:3, :] = jnp.sum(mg * attend_sum, axis=0, keepdims=True)
    sums[3:4, :] = jnp.sum(ac.astype(F32), axis=0, keepdims=True)


def middle_back(x, own, other, outer_bias, gate_attend, scale, grad_own, grad_other, cot, outer, upper, before, block=256):
    tok, width = x.shape
    local = outer.shape[0]
    blocks = tok // block
    start = blocks if upper else 0
    row = pl.BlockSpec((block, width), lambda i: (i, 0))
    at = lambda cols: pl.BlockSpec((block, cols), lambda i: (i + start, 0))
    vec = whole((1, width))
    return pl.pallas_call(
        middle_body,
        grid=(blocks,),
        in_specs=[row, row, row, vec, vec, vec, row, row, row, whole(outer.shape)]
        + [pl.BlockSpec(memory_space=pl.ANY)] * len(before),
        out_specs=[row, at(width), at(local), pl.BlockSpec((None, 8, width), lambda i: (i, 0, 0))],
        out_shape=[
            jax.ShapeDtypeStruct((tok, width), F32),
            jax.ShapeDtypeStruct((2 * tok, width), BF16),
            jax.ShapeDtypeStruct((2 * tok, local), BF16),
            jax.ShapeDtypeStruct((blocks, 8, width), F32),
        ],
        input_output_aliases={10 + i: 1 + i for i in range(len(before))},
        compiler_params=params("arbitrary"),
        cost_estimate=cost(2 * tok * width * local, 26 * tok * width),
        name="middle_back",
    )(x, own, other, outer_bias, gate_attend, scale, grad_own, grad_other, cot, outer, *before)


def spread_body(*refs):
    parts, weight, out = refs[:-2], refs[-2], refs[-1]
    total = None
    for j in range(3):
        grads = jnp.concatenate([part[j] for part in parts], axis=1)
        grown = mm(grads, weight[j], NT)
        total = grown if total is None else total + grown
    out[...] = total


def spread(parts, weight, first, count, block=256):
    local = weight.shape[2]
    width = weight.shape[1]
    some = lambda part: pl.BlockSpec((3, block, part.shape[2]), lambda i: (0, i + first // block, 0))
    return pl.pallas_call(
        spread_body,
        grid=(count // block,),
        in_specs=[some(part) for part in parts] + [whole(weight.shape)],
        out_specs=pl.BlockSpec((block, width), lambda i: (i, 0)),
        out_shape=jax.ShapeDtypeStruct((count, width), F32),
        compiler_params=params("arbitrary"),
        cost_estimate=cost(6 * count * local * width, 6 * (count * local + local * width) + 4 * count * width),
        name="spread",
    )(*parts, weight)


def final_body(x, scale, own, other, middle_grad, frames_grad, sums):
    unit, inverse = normalise(x[...].astype(F32))
    grad = own[...] + other[...]
    frames_grad[...] = middle_grad[...] + norm_back(grad, unit, inverse, scale[...])
    sums[...] = jnp.zeros_like(sums)
    sums[0:1, :] = jnp.sum(grad, axis=0, keepdims=True)
    sums[1:2, :] = jnp.sum(grad * unit, axis=0, keepdims=True)


def final_back(x, scale, own, other, middle_grad):
    rows, width = x.shape
    block = min(256, rows)
    blocks = rows // block
    row = pl.BlockSpec((block, width), lambda i: (i, 0))
    return pl.pallas_call(
        final_body,
        grid=(blocks,),
        in_specs=[row, whole((1, width)), row, row, row],
        out_specs=[row, pl.BlockSpec((None, 8, width), lambda i: (i, 0, 0))],
        out_shape=[jax.ShapeDtypeStruct((rows, width), F32), jax.ShapeDtypeStruct((blocks, 8, width), F32)],
        compiler_params=params("arbitrary"),
        cost_estimate=cost(20 * rows * width, 16 * rows * width),
        name="final_back",
    )(x, scale, own, other, middle_grad)


def cross(values, mask):
    return lax.ppermute(values, "dp", [(i, i ^ mask) for i in range(16)])


def crossed(sends):
    return [cross(values, mask) for values, mask in sends]


class Reduce:
    def __init__(self, values, index):
        self.index = index
        cols = values[0].shape[-1]
        self.values = [v.reshape(-1, 4, 4, v.shape[-2] // 16, cols) for v in values]
        self.rows = self.values[0].shape[3] // 2

    def take(self, mask):
        at = (self.index % 4) ^ mask
        return [lax.dynamic_index_in_dim(v, at, 2, keepdims=False) for v in self.values]

    def first(self):
        far, rows = self.take(3), self.rows
        pack = lambda part: jnp.concatenate([f[:, :, part].astype(BF16) for f in far], axis=0)
        return [(pack(slice(0, rows)), 1), (pack(slice(rows, None)), 2)]

    def second(self, got):
        rows = self.rows
        joined = lambda mask: jnp.concatenate(self.take(mask), axis=0)
        to_x, to_y = joined(1), joined(2)
        none = jnp.zeros_like(got[0])
        to_x = (to_x + jnp.concatenate([none, got[1]], axis=2).astype(F32)).astype(BF16)
        to_y = (to_y + jnp.concatenate([got[0], none], axis=2).astype(F32)).astype(BF16)
        return [(to_x, 1), (to_y, 2)]

    def third(self, got):
        self.near = jnp.concatenate(self.take(0), axis=0) + (got[0].astype(F32) + got[1].astype(F32))
        at = self.index // 4
        block = lambda mask: lax.dynamic_index_in_dim(self.near, at ^ mask, 1, keepdims=False)
        self.own = block(0)
        return [(block(mask).astype(BF16), 4 * mask) for mask in (1, 2, 3)]

    def last(self, got):
        got = [g.astype(F32) for g in got]
        return ((self.own + got[0]) + (got[1] + got[2])).astype(BF16)


def cut_columns(values, cols):
    return jnp.concatenate([values[..., at : at + cols] for at in range(0, values.shape[-1], cols)], axis=0)


def joined(sends, more):
    return [(jnp.concatenate([values, more], axis=0), mask) for values, mask in sends]


def split(got, count):
    return [g[:count] for g in got], [g[count:] for g in got]


class Spread:
    def __init__(self, own):
        self.own = own

    def first(self):
        return [(self.own, 1), (self.own, 2)]

    def second(self, got):
        self.side = got
        rows = self.own.shape[2] // 2
        return [(got[1][:, :, :rows], 1), (got[0][:, :, rows:], 2)]

    def parts(self, got):
        return (self.own, *self.side, *got)


def placed(index, refs):
    own, side_x, side_y, far_low, far_high = refs
    rows = own.shape[1]
    half = rows // 2
    here = index[0] % 4
    return [
        (here, slice(0, rows), own),
        (here ^ 1, slice(0, rows), side_x),
        (here ^ 2, slice(0, rows), side_y),
        (here ^ 3, slice(0, half), far_low),
        (here ^ 3, slice(half, rows), far_high),
    ]


def assemble_heads_body(index, *refs):
    inner, outer = refs[5:]
    cols = refs[0].shape[2]
    for at, span, ref in placed(index, refs[:5]):
        inner[:, at, span, :cols] = ref[0:3].astype(F32)
        inner[:, at, span, cols:] = ref[5:8].astype(F32)
        outer[at, span, :cols] = ref[3].astype(F32)
        outer[at, span, cols:] = ref[4].astype(F32)


def assemble_feed_body(index, *refs):
    cols = refs[0].shape[2]
    for at, span, ref in placed(index, refs[:5]):
        for part in range(8):
            refs[5 + part % 2][at, span, (part // 2) * cols : (part // 2 + 1) * cols] = ref[part].astype(F32)


def assemble(body, index, parts, out_specs, out_shape):
    _, count, rows, cols = parts[0].shape
    spec = lambda r: pl.BlockSpec(
        (None, count, r, cols), lambda z, index: (z ^ (index[0] // 4), 0, 0, 0)
    )
    return pl.pallas_call(
        body,
        grid_spec=pltpu.PrefetchScalarGridSpec(
            num_scalar_prefetch=1,
            grid=(4,),
            in_specs=[spec(rows)] * 3 + [spec(rows // 2)] * 2,
            out_specs=out_specs,
        ),
        out_shape=[jax.ShapeDtypeStruct(shape, F32) for shape in out_shape],
        compiler_params=params("arbitrary"),
        cost_estimate=cost(0, 6 * count * 16 * rows * cols),
        name="assemble",
    )(index[None], *parts)


def assemble_heads(index, *parts):
    _, count, rows, cols = parts[0].shape
    inner, outer = assemble(
        assemble_heads_body, index, parts,
        [
            pl.BlockSpec((3, 4, rows, 2 * cols), lambda z, index: (0, z, 0, 0)),
            pl.BlockSpec((4, rows, 2 * cols), lambda z, index: (z % 2, 0, z // 2)),
        ],
        [(3, 16, rows, 2 * cols), (8, rows, 4 * cols)],
    )
    return inner.reshape(3, 16 * rows, 2 * cols), outer.reshape(8 * rows, 4 * cols)


def assemble_feed(index, *parts):
    _, count, rows, cols = parts[0].shape
    outs = assemble(
        assemble_feed_body, index, parts,
        [pl.BlockSpec((4, rows, 4 * cols), lambda z, index: (z, 0, 0))] * 2,
        [(16, rows, 4 * cols)] * 2,
    )
    return [out.reshape(16 * rows, 4 * cols) for out in outs]


def tie(*groups):
    leaves, tree = jax.tree.flatten(groups)
    held = iter(lax.optimization_barrier(tuple(v for v in leaves if hasattr(v, "dtype"))))
    return jax.tree.unflatten(tree, [next(held) if hasattr(v, "dtype") else v for v in leaves])


def fold(parts):
    while parts.shape[0] > 1:
        parts = parts[0::2] + parts[1::2]
    return parts[0]


def tables(lengths, row_len, offset):
    frame_index = (jnp.arange(row_len, dtype=jnp.int32) + offset) % row_len
    seg_ends = jnp.cumsum(lengths)
    segment = jnp.sum((frame_index[:, None] >= seg_ends[None, :]).astype(jnp.int32), axis=1)
    starts = seg_ends - lengths
    picked = jnp.arange(lengths.shape[0], dtype=jnp.int32)[None, :] == segment[:, None]
    before = jnp.sum(jnp.where(picked, starts[None, :], 0), axis=1)
    position = (frame_index - before).astype(F32)
    half = HEAD_DIM // 2
    lane = jnp.arange(PAIR, dtype=jnp.int32)
    frequency = 10000.0 ** (-(lane % half).astype(F32) / half)
    sign = jnp.where(lane % HEAD_DIM < half, -1.0, 1.0).astype(F32)
    angles = position[:, None] * frequency[None, :]
    return segment, jnp.cos(angles), jnp.sin(angles) * sign[None, :]


def per_device(
    frames, time_embed, seg_lengths, mod_weight, mod_bias, inner_weight, inner_bias, outer_weight,
    outer_bias, up_weight, up_bias, down_weight, down_bias, cotangent,
):
    own_tok, width = frames.shape
    group = lax.axis_size("tensor")
    size = lax.axis_size("dp")
    index = lax.axis_index("dp")
    rank = lax.axis_index("tensor")
    rows = own_tok * group
    tok = rows // 2
    paired = group == 2
    staged = size == 16
    pairs = inner_weight.shape[2] // PAIR
    swap = lambda v: lax.ppermute(v, "tensor", [(0, 1), (1, 0)])

    def halves(values):
        if paired:
            return values, swap(values)
        full = lax.all_gather(values, "tensor", axis=0, tiled=True)
        return full[:tok], full[tok:]

    def summed(low, high):
        if paired:
            other_low, other_high = swap(high), swap(low)
            return (low, other_low), (high, other_high)
        low, high = lax.psum((low, high), "tensor")
        none = jnp.zeros_like(low)
        return (low, none), (high, none)

    def own_rows(low, high):
        full = jnp.concatenate([low, high], axis=0)
        return lax.dynamic_slice_in_dim(full, rank * own_tok, own_tok, 0)

    def tensor_sum(values):
        return values + swap(values) if paired else lax.psum(values, "tensor")

    x_low, x_high = halves(frames)
    cot_low, cot_high = halves(cotangent)
    segment, cosine, sine = tables(seg_lengths[0], rows, rank * tok if paired else 0)
    seg_col, seg_row = segment[:, None], segment[None, :]
    acted = jax.nn.silu(time_embed.astype(F32)).astype(BF16)
    mod_part = jnp.dot(acted, mod_weight, preferred_element_type=F32) + mod_bias.astype(F32)
    if paired:
        other = swap(mod_part)
        first = rank == 0
        modulation = jnp.concatenate(
            [jnp.where(first, mod_part, other), jnp.where(first, other, mod_part)], axis=1
        )
    else:
        modulation = lax.all_gather(mod_part, "tensor", axis=1, tiled=True)
    shift_attend, scale_attend, gate_attend, shift_feed, scale_feed, gate_feed = [
        modulation[:, column * width : (column + 1) * width] for column in range(6)
    ]
    normed, queries, keys, vals = project(
        x_low, x_high, shift_attend, scale_attend, inner_weight, inner_bias.astype(F32), cosine, sine
    )
    mixed, logs, part_low, part_high = attend(queries, keys, vals, seg_col, seg_row, outer_weight)
    (own_low, other_low), (own_high, other_high) = summed(part_low, part_high)
    outer_vec = outer_bias.astype(F32)[None, :]
    feed_rest = (
        outer_vec, gate_attend, shift_feed, scale_feed, gate_feed,
        up_weight, up_bias.astype(F32)[None, :], down_weight,
    )
    *shared, feed_low, grad_low, sums_low = feed(
        x_low, own_low, other_low, *feed_rest, cot_low, None
    )
    *shared, feed_high, grad_high, sums_high = feed(
        x_high, own_high, other_high, *feed_rest, cot_high, shared
    )
    normed_feed, active, lift_grad, feed_cot = shared
    feed_vec = fold(jnp.concatenate([sums_low, sums_high]))
    (grad_low, grad_low_other), (grad_high, grad_high_other) = summed(grad_low, grad_high)
    down_grad = mm(active, feed_cot, TN)
    up_grad = mm(normed_feed, lift_grad, TN)
    middle_rest = (outer_vec, gate_attend, scale_feed)

    if staged:
        one = Reduce([down_grad, up_grad], index)
        sends = one.first()
        grad_low_other, sends = tie(grad_low_other, sends)
        got = crossed(sends)
    middle_high, *shared, vec_high = middle_back(
        x_high, own_high, other_high, *middle_rest, grad_high, grad_high_other, cot_high,
        outer_weight, True, [],
    )
    middle_low, attend_cot, heads_grad, vec_low = middle_back(
        x_low, own_low, other_low, *middle_rest, grad_low, grad_low_other, cot_low,
        outer_weight, False, shared,
    )
    if staged:
        middle_low, attend_cot, heads_grad, vec_low, vec_high, got = tie(
            middle_low, attend_cot, heads_grad, vec_low, vec_high, got
        )
        sends = one.second(got)
    middle_vec = fold(jnp.concatenate([vec_low, vec_high]))
    outer_grad = mm(mixed, attend_cot, TN)

    back = lambda grads, *where: attend_back(
        queries, keys, vals, grads, logs, seg_col, seg_row, cosine, sine, *where
    )
    inner_grad = lambda part: [mm(normed, part[j], TN) for j in range(3)]
    if staged:
        early = pairs // 2
        heads_grad, sends = tie(heads_grad, sends)
        got = crossed(sends)
        near = back(heads_grad, 0, early, early, 0)
        near, got = tie(near, got)
        sends = one.third(got)
        cols = [outer_grad[:, at : at + early * PAIR] for at in range(0, width, early * PAIR)]
        cols = [jnp.concatenate([cols[at], cols[at + 2]], axis=0) for at in (0, 1)]
        two = Reduce(inner_grad(near[0]) + cols, index)
        sends2 = two.first()
        heads_grad, sends, sends2 = tie(heads_grad, sends, sends2)
        got, got2 = crossed(sends), crossed(sends2)
        late = pairs - early
        far = back(heads_grad, early, late // 2, late, 0)
        far, got2, got[1] = tie(far, got2, got[1])
        sends2 = two.second(got2)
        heads_grad, sends2 = tie(heads_grad, sends2)
        got2 = crossed(sends2)
        far = back(heads_grad, early + late // 2, late - late // 2, late, late // 2, far)
        far, got, got2 = tie(far, got, got2)
        mine1 = cut_columns(one.last(got), early * PAIR)
        sends2 = joined(two.third(got2), mine1)
        three = Reduce(inner_grad(far[0]), index)
        sends3 = three.first()
        results = [near, far]
    else:
        results = [back(heads_grad, 0, pairs, pairs, 0)]
        inner_grads = inner_grad(results[0][0])
    parts = [part for part, _ in results]
    part_sums = jnp.concatenate([sums for _, sums in results], axis=1)

    if staged:
        parts[-1], sends2, sends3, feed_low, feed_high = tie(
            parts[-1], sends2, sends3, feed_low, feed_high
        )
        got3, got2 = crossed(sends3), crossed(sends2)
    if paired:
        spread_other = spread(parts, inner_weight, tok, tok)
        if staged:
            spread_other, got3 = tie(spread_other, got3)
            sends3 = three.second(got3)
            parts[-1], sends3 = tie(parts[-1], sends3)
            got3 = crossed(sends3)
        spread_other = swap(spread_other)
        spread_own = spread(parts, inner_weight, 0, tok)
        own_middle = middle_low
    else:
        both = lax.psum(spread(parts, inner_weight, 0, rows), "tensor")
        spread_own = own_rows(both[:tok], both[tok:])
        spread_other = jnp.zeros_like(spread_own)
        own_middle = own_rows(middle_low, middle_high)
    if staged:
        spread_own, got2, got3 = tie(spread_own, got2, got3)
        got2, got1 = split(got2, two.own.shape[0])
        mine2 = two.last(got2)
        feed_grads = Spread(jnp.stack([mine1] + got1))
        sends1 = feed_grads.first()
        sends3 = joined(three.third(got3), mine2)
        spread_own, sends1, sends3, feed_low = tie(spread_own, sends1, sends3, feed_low)
        got3, got1 = crossed(sends3), crossed(sends1)
    frames_grad, final_sums = final_back(frames, scale_attend, spread_own, spread_other, own_middle)
    if staged:
        frames_grad, final_sums, got3 = tie(frames_grad, final_sums, got3)
        got3, got2 = split(got3, three.own.shape[0])
        mine3 = three.last(got3)
        _, got1 = tie(mine3, got1)
        got3 = crossed([(mine3, 4 * mask) for mask in (1, 2, 3)])

    if paired:
        feed_sum = feed_low + swap(feed_high)
        attend_sum = own_low + other_low + outer_vec
    else:
        feed_sum = own_rows(*lax.psum((feed_low, feed_high), "tensor"))
        attend_sum = own_rows(own_low, own_high) + outer_vec
    feed_sum = feed_sum + down_bias.astype(F32)[None, :]
    output = (frames.astype(F32) + gate_attend * attend_sum + gate_feed * feed_sum).astype(BF16)

    final_vec = fold(final_sums)

    crossing = tensor_sum(jnp.concatenate([final_vec[0:1], final_vec[1:2], feed_vec[0:1]], axis=1))
    gate_feed_grad = crossing[:, 2 * width :] + down_bias.astype(F32)[None, :] * feed_vec[3:4]
    mod_full = jnp.concatenate(
        [crossing[:, : 2 * width], middle_vec[2:3], middle_vec[0:1], middle_vec[1:2], gate_feed_grad],
        axis=1,
    )
    share = mod_weight.shape[1]
    local = inner_weight.shape[2]
    units = up_weight.shape[1]
    mod_grad = lax.dynamic_slice_in_dim(mod_full, rank * share, share, 1).astype(BF16)
    inner_biases = [part_sums[j] for j in range(3)]
    biases = jnp.concatenate(inner_biases + [feed_vec[2, :units], middle_vec[3], feed_vec[1]])
    small = jnp.concatenate([acted.astype(F32), mod_grad.astype(F32), biases[None, :]], axis=1)
    if staged:
        near = jnp.concatenate([small] + [cross(small, mask) for mask in (1, 2, 3)], axis=0)
        small = jnp.concatenate([near] + [cross(near, 4 * mask) for mask in (1, 2, 3)], axis=0)
        slot = jnp.arange(size, dtype=jnp.int32)
        order = ((slot[:, None] ^ index) == slot[None, :]).astype(BF16)
        factors = mm(order, small[:, : width + share].astype(BF16)).astype(BF16)
        biases = fold(small[:, width + share :][:, None, :])[0]
    else:
        small = lax.all_gather(small, "dp", axis=0, tiled=True)
        factors = small[:, : width + share].astype(BF16)
        biases = jnp.sum(small[:, width + share :], axis=0)
    all_acted, all_mod = factors[:, :width], factors[:, width:]
    mod_weight_grad = mm(all_acted, all_mod, TN)
    mod_bias_grad = jnp.sum(all_mod.astype(F32), axis=0)
    acted_grad = tensor_sum(mm(mod_grad, mod_weight, NT))
    time_grad = jax.vjp(jax.nn.silu, time_embed.astype(F32))[1](acted_grad)[0]

    if staged:
        got1 = crossed(feed_grads.second(got1))
        both = lambda a, b: jnp.concatenate([a, b], axis=0)
        head_grads = Spread(jnp.stack([both(mine2, mine3)] + [both(a, b) for a, b in zip(got2, got3)]))
        sends = head_grads.first()
        _, got1 = tie(sends, got1)
        got = crossed(sends)
        down_total, up_total = assemble_feed(index, *feed_grads.parts(got1))
        got = crossed(head_grads.second(got))
        inner_total, outer_total = assemble_heads(index, *head_grads.parts(got))
    else:
        inner_total = jnp.stack(inner_grads)
        down_total, up_total, outer_total, inner_total = lax.psum(
            (down_grad, up_grad, outer_grad, inner_total), "dp"
        )

    cut = 3 * local
    return (
        output,
        frames_grad,
        time_grad,
        mod_weight_grad,
        mod_bias_grad,
        inner_total,
        biases[:cut].reshape(3, local),
        outer_total,
        biases[cut + units : cut + units + width],
        up_total,
        biases[cut : cut + units],
        down_total,
        biases[cut + units + width :],
    )


def solution(mesh):
    in_specs = (
        P(("dp", "tensor"), None),
        P("dp", None),
        P("dp", None),
        P(None, "tensor"),
        P("tensor"),
        P(None, None, "tensor"),
        P(None, "tensor"),
        P("tensor", None),
        P(),
        P(None, "tensor"),
        P("tensor"),
        P("tensor", None),
        P(),
        P(("dp", "tensor"), None),
    )
    out_specs = (
        P(("dp", "tensor"), None),
        P(("dp", "tensor"), None),
        P("dp", None),
        P(None, "tensor"),
        P("tensor"),
        P(None, None, "tensor"),
        P(None, "tensor"),
        P("tensor", None),
        P(),
        P(None, "tensor"),
        P("tensor"),
        P("tensor", None),
        P(),
    )
    return jax.shard_map(
        per_device, mesh=mesh, in_specs=in_specs, out_specs=out_specs, check_vma=False
    )
```
